128 devices in a mesh: gx: 8 (over y, core), gy: 16 (over x, z).
Axes of the slice: x: 4, y: 4, z: 4, core: 2. Of those that a mesh axis runs over, the one named last changes fastest.
Arguments:
- owned_surplus: float32 [16384, 16, 256], P(('gx', 'gy')), may hold values from -0.6 to 0.6
- tile_owner: int32 [16384], replicated, may hold values from 0 to 127, as said below
- grid_levels: int32 [8, 2], replicated, may hold values from 0 to 3, as said below
- coefficients: int32 [8], replicated, may hold values from 1 to 3
- faulty_grids: int32 [2], replicated, may hold values from 1 to 7
- velocity_x: float32 [4096, 16384], P('gx', 'gy'), may hold values from -1 to 1
- velocity_y: float32 [4096, 16384], P('gx', 'gy'), may hold values from -1 to 1
Outputs:
- solution: float32 [4096, 16384], P('gx', 'gy')
The draws below stay inside these ranges and needn't reach their ends.
Inputs may be any that keep to these rules, and one draw needn't show every extreme that they name: tile_owner[d * 128 + k] = (d + o_k) mod (the number of devices), with offsets o_k that depend only on k; no offset value serves more than 2 of the 128 values of k, and some offset value serves exactly 2. `grid_levels`: row 0 is (0, 0), the full grid.
All inputs are finite; a program needn't handle non-finite values.
Results may differ from the reference program's by a relative error of at most 0.00011.
Values sent between devices are 32-bit elements; how exact they have to be, the bound alone decides.
No kernel may reach another device: no remote copies, remote signals or barrier semaphores. Data moves between devices by JAX's collectives and lax.ppermute only.
A program may use at most 128 MiB of HBM per device.

```python
import jax
import jax.numpy as jnp
import numpy as np
from jax import lax

CX = 512
CY = 1024
TILE_ROWS = 32
TILE_COLS = 4
GRIDS = 8
FAULTS = 2
STEPS = 2
SLOTS = 128
TX = 16
TY = 256
NX = 4096
NY = 16384
DEVICES = 128


def draw_tile_owner(key, part):
    device_total = NX // CX * (NY // CY)
    capacity = 2 * SLOTS // device_total
    quarter = device_total // 4
    counts_list = [capacity] * quarter + [capacity // 2] * (2 * quarter) + [0] * (device_total - 3 * quarter)
    rank_of_slot = np.repeat(np.arange(device_total), np.array(counts_list))
    order_values = jax.random.permutation(jax.random.fold_in(key, 11), device_total)
    offsets = order_values[jnp.asarray(rank_of_slot, dtype=jnp.int32)]
    offsets = jax.random.permutation(jax.random.fold_in(key, 12), offsets)
    dest_ids = jnp.arange(device_total, dtype=jnp.int32)[:, None]
    return ((dest_ids + offsets[None, :]) % device_total).reshape(-1).astype(jnp.int32)


def draw_grid_levels(key, part):
    drops = jax.random.randint(jax.random.fold_in(key, 21), (GRIDS, 2), 0, 4)
    drops = drops.at[0].set(0)
    drops = drops.at[1, 0].set(3)
    return drops.astype(jnp.int32)


def with_ends(values, stream_key, low, high):
    spot = [jax.random.randint(jax.random.fold_in(stream_key, axis), (), 0, length) for axis, length in enumerate(values.shape)]
    longest = values.shape.index(max(values.shape))
    neighbour = spot[:longest] + [(spot[longest] + 1) % values.shape[longest]] + spot[longest + 1:]
    return values.at[tuple(spot)].set(low).at[tuple(neighbour)].set(high)


def block_levels(rng, shape, pieces, least, high):
    gain = 1.0
    for position, blocks in pieces:
        steps = jax.random.uniform(jax.random.fold_in(jax.random.fold_in(rng, 6), position), (blocks,), jnp.float32, least / len(pieces), high / len(pieces))
        gain = gain * jnp.repeat(jnp.exp(steps), shape[position] // blocks).reshape((-1,) + (1,) * (len(shape) - 1 - position))
    return gain


def normal_values(stream_key, shape, width, reach, cuts=(), kind=jnp.bfloat16):
    level = block_levels(stream_key, shape, cuts, -0.22, 0.18) if cuts else 1.0
    values = jax.random.normal(stream_key, shape, jnp.float32) * width * level
    return jnp.minimum(jnp.maximum(values, -reach), reach).astype(kind)


def setup_inputs(seed: int = 0) -> dict:
    keys = jax.random.split(jax.random.key(seed), 8)
    return {
        "owned_surplus": normal_values(keys[0], (DEVICES * SLOTS, TX, TY), 0.1, 0.6, ((0, 128),), jnp.float32),
        "tile_owner": draw_tile_owner(jax.random.fold_in(keys[7], 71), 0),
        "grid_levels": draw_grid_levels(jax.random.fold_in(keys[7], 71), 0),
        "coefficients": with_ends(jax.random.randint(keys[3], (GRIDS,), 1, 4), jax.random.fold_in(keys[3], 1), 1, 3).astype(jnp.int32),
        "faulty_grids": jax.random.randint(keys[4], (FAULTS,), 1, GRIDS).astype(jnp.int32),
        "velocity_x": jnp.clip(jax.random.uniform(keys[5], (NX, NY), jnp.float32, -1.0, 1.0) * block_levels(keys[5], (NX, NY), ((0, 8), (1, 16)), -0.4, 0.0), -1.0, 1.0),
        "velocity_y": jnp.clip(jax.random.uniform(keys[6], (NX, NY), jnp.float32, -1.0, 1.0) * block_levels(keys[6], (NX, NY), ((0, 8), (1, 16)), -0.4, 0.0), -1.0, 1.0),
    }


TIME_STEP = 0.2
DIFFUSION = 0.5


def level_of(index_row, top_level):
    result = jnp.full(index_row.shape, top_level, jnp.int32)
    for bit_pos in range(1, top_level + 1):
        result = jnp.where(index_row % (2 ** bit_pos) == 0, top_level - bit_pos, result)
    return result


def weight_table(grid_levels, coefficients, faulty_grids, top_x, top_y):
    grid_count = coefficients.shape[0]
    grid_ids = jnp.arange(grid_count, dtype=jnp.int32)
    alive_mask = jnp.all(faulty_grids[None, :] != grid_ids[:, None], axis=1)
    grid_share = jnp.where(alive_mask, coefficients, 0).astype(jnp.float32)
    covers_x = (jnp.arange(top_x + 1, dtype=jnp.int32)[:, None] <= (top_x - grid_levels[None, :, 0])).astype(jnp.float32)
    covers_y = (jnp.arange(top_y + 1, dtype=jnp.int32)[:, None] <= (top_y - grid_levels[None, :, 1])).astype(jnp.float32)
    return jnp.dot(covers_x * grid_share[None, :], covers_y.T, precision=lax.Precision.HIGHEST)


def refine(values, ends_next):
    spacing = values.shape[0] // 2
    while spacing >= 1:
        corners = jnp.concatenate([values[0::2 * spacing], ends_next], axis=0)
        middle = values[spacing::2 * spacing]
        values = values.at[spacing::2 * spacing].set(middle + 0.5 * (corners[:-1] + corners[1:]))
        spacing = spacing // 2
    return values


def rates(padded, vel_x, vel_y):
    centre = padded[2:-2, 2:-2]
    east_one = padded[3:-1, 2:-2]
    west_one = padded[1:-3, 2:-2]
    east_two = padded[4:, 2:-2]
    west_two = padded[:-4, 2:-2]
    north_one = padded[2:-2, 3:-1]
    south_one = padded[2:-2, 1:-3]
    north_two = padded[2:-2, 4:]
    south_two = padded[2:-2, :-4]
    slope_x = (8.0 * (east_one - west_one) - (east_two - west_two)) / 12.0
    slope_y = (8.0 * (north_one - south_one) - (north_two - south_two)) / 12.0
    curve_x = (16.0 * (east_one + west_one) - (east_two + west_two) - 30.0 * centre) / 12.0
    curve_y = (16.0 * (north_one + south_one) - (north_two + south_two) - 30.0 * centre) / 12.0
    return DIFFUSION * (curve_x + curve_y) - vel_x * slope_x - vel_y * slope_y


def reference(owned_surplus, tile_owner, grid_levels, coefficients, faulty_grids, velocity_x, velocity_y):
    tile_index = jnp.arange(tile_owner.shape[0], dtype=jnp.int32)
    source_rows = (tile_owner * SLOTS + tile_index % SLOTS).astype(jnp.int32)
    tile_data = jnp.take(owned_surplus, source_rows, axis=0)
    blocks_x = NX // CX
    blocks_y = NY // CY
    grid = tile_data.reshape(blocks_x, blocks_y, TILE_ROWS, TILE_COLS, TX, TY)
    grid = grid.transpose(0, 2, 4, 1, 3, 5).reshape(NX, NY)
    top_x = int(NX).bit_length() - 1
    top_y = int(NY).bit_length() - 1
    table = weight_table(grid_levels, coefficients, faulty_grids, top_x, top_y)
    levels_x = level_of(jnp.arange(NX, dtype=jnp.int32), top_x)
    levels_y = level_of(jnp.arange(NY, dtype=jnp.int32), top_y)
    weights = jnp.take(jnp.take(table, levels_x, axis=0), levels_y, axis=1)
    surplus = grid * weights
    nodal_x = refine(surplus, surplus[0:1])
    flipped = nodal_x.T
    nodal = refine(flipped, flipped[0:1]).T
    field_now = nodal
    for step_index in range(STEPS):
        first_rate = rates(jnp.pad(field_now, 2, mode="wrap"), velocity_x, velocity_y)
        middle_field = field_now + TIME_STEP * first_rate
        second_rate = rates(jnp.pad(middle_field, 2, mode="wrap"), velocity_x, velocity_y)
        field_now = 0.5 * (field_now + middle_field + TIME_STEP * second_rate)
    return field_now
```

```python
import functools

import jax
import jax.numpy as jnp
from jax import lax
from jax.experimental import pallas as pl
from jax.experimental.pallas import tpu as pltpu
from jax.sharding import PartitionSpec as P

STEPS = 2
TIME_STEP = 0.2
DIFFUSION = 0.5
HALO = 8
LANES = 128
HAT = 256
VMEM_LIMIT = 48 << 20


def pack_kernel(slots_ref, owned_ref, outgoing_ref, staged, sem_in, sem_out):
    count = owned_ref.shape[0]
    whole = pltpu.make_async_copy(owned_ref, staged, sem_in)
    whole.start()
    whole.wait()

    def send(k, carry):
        pltpu.make_async_copy(staged.at[k], outgoing_ref.at[slots_ref[k]], sem_out).start()
        return carry

    lax.fori_loop(0, count, send, 0)
    pltpu.make_async_copy(staged, outgoing_ref.at[pl.ds(0, count)], sem_out).wait()


def pack(slots, owned, capacity):
    count = owned.shape[0]
    return pl.pallas_call(
        pack_kernel,
        out_shape=jax.ShapeDtypeStruct((count * capacity,) + owned.shape[1:], owned.dtype),
        in_specs=[pl.BlockSpec(memory_space=pltpu.SMEM), pl.BlockSpec(memory_space=pl.ANY)],
        out_specs=pl.BlockSpec(memory_space=pl.ANY),
        scratch_shapes=[
            pltpu.VMEM(owned.shape, owned.dtype),
            pltpu.SemaphoreType.DMA,
            pltpu.SemaphoreType.DMA,
        ],
        name="pack_tiles",
    )(slots, owned)


def split_dot(left, right, split_left):
    value = left if split_left else right
    high = value.astype(jnp.bfloat16)
    low = (value - high.astype(jnp.float32)).astype(jnp.bfloat16)
    if split_left:
        pairs = ((high, right), (low, right))
    else:
        pairs = ((left, high), (left, low))
    return sum(jnp.dot(a, b, preferred_element_type=jnp.float32) for a, b in pairs)


def refine_kernel(
    tiles_down, tiles_across, slots_ref, incoming_ref, weight_ref, hat_x_ref, hat_y_ref, rows_ref,
    cols_ref, nodal_ref, left_ref, right_ref, block, sem,
):
    count = tiles_down * tiles_across
    tile_rows, tile_cols = incoming_ref.shape[1:]
    height = tiles_down * tile_rows

    def fetch(kx, carry):
        for ky in range(tiles_across):
            pltpu.make_async_copy(
                incoming_ref.at[slots_ref[kx * tiles_across + ky]],
                block.at[pl.ds(pl.multiple_of(kx * tile_rows, tile_rows), tile_rows),
                         pl.ds(ky * tile_cols, tile_cols)],
                sem,
            ).start()
        return carry

    lax.fori_loop(0, tiles_down, fetch, 0)
    pltpu.make_async_copy(block, block, sem).wait()

    weight = jnp.concatenate([weight_ref[...]] * (HAT // LANES), axis=1)[None]
    row_id = lax.broadcasted_iota(jnp.int32, (HAT, HAT), 0)
    lane_id = lax.broadcasted_iota(jnp.int32, (HAT, HAT), 1)
    ramp_rows = row_id.astype(jnp.float32) * (1.0 / HAT)
    ramp_lanes = lane_id.astype(jnp.float32) * (1.0 / HAT)
    for ky in range(tiles_across):
        lanes = slice(ky * HAT, (ky + 1) * HAT)
        own = rows_ref[0:1, lanes]
        after = rows_ref[1:2, lanes]
        middle = block[HAT : HAT + 1, lanes] * weight[0, 0:1] + 0.5 * (own + after)
        for part, (first, last) in enumerate(((own, middle), (middle, after))):
            rows = slice(part * HAT, (part + 1) * HAT)
            values = (block[rows, lanes].reshape(HAT // 8, 8, HAT) * weight).reshape(HAT, HAT)
            values = jnp.where(row_id == 0, first, values)
            block[rows, lanes] = split_dot(hat_x_ref[...], values, False) + ramp_rows * last
    for part in range(height // HAT):
        rows = slice(part * HAT, (part + 1) * HAT)
        ends = [cols_ref[rows, 0:1], None, None, None, cols_ref[rows, 1:2]]
        for middle, before, after in ((2, 0, 4), (1, 0, 2), (3, 2, 4)):
            ends[middle] = block[rows, middle * HAT : middle * HAT + 1] + 0.5 * (
                ends[before] + ends[after]
            )
        for ky in range(tiles_across):
            values = jnp.where(lane_id == 0, ends[ky], block[rows, ky * HAT : (ky + 1) * HAT])
            result = split_dot(values, hat_y_ref[...], True) + ramp_lanes * ends[ky + 1]
            nodal_ref[2 * ky, rows, :] = result[:, :LANES]
            nodal_ref[2 * ky + 1, rows, :] = result[:, LANES:]
            if ky == 0:
                left_ref[:, rows] = result[:, :LANES].T[:HALO]
            if ky == tiles_across - 1:
                right_ref[:, rows] = result[:, LANES:].T[-HALO:]


def refine_block(slots, incoming, weight, hat_x, hat_y, rows, cols, height, width):
    tile_rows, tile_cols = incoming.shape[1:]
    vmem = pl.BlockSpec(memory_space=pltpu.VMEM)
    return pl.pallas_call(
        functools.partial(refine_kernel, height // tile_rows, width // tile_cols),
        out_shape=(
            jax.ShapeDtypeStruct((width // LANES, height, LANES), jnp.float32),
            jax.ShapeDtypeStruct((HALO, height), jnp.float32),
            jax.ShapeDtypeStruct((HALO, height), jnp.float32),
        ),
        in_specs=[pl.BlockSpec(memory_space=pltpu.SMEM), pl.BlockSpec(memory_space=pl.ANY)]
        + [vmem] * 5,
        out_specs=(vmem, vmem, vmem),
        scratch_shapes=[pltpu.VMEM((height, width), jnp.float32), pltpu.SemaphoreType.DMA],
        compiler_params=pltpu.CompilerParams(vmem_limit_bytes=VMEM_LIMIT),
        name="refine_block",
    )(slots, incoming, weight, hat_x, hat_y, rows, cols)


def fill_halo(target, height, width, above, below, left, right):
    tiles = width // LANES
    first = 2 * HALO
    for t in range(tiles):
        target[t, HALO:first, :] = above[:, t * LANES : (t + 1) * LANES]
        target[t, first + height : first + height + HALO, :] = below[:, t * LANES : (t + 1) * LANES]
    between = jnp.zeros((LANES - 2 * HALO, height), jnp.float32)
    sides = jnp.concatenate([right[:, :height], between, left[:, :height]], axis=0)
    target[tiles, first : first + height, :] = sides.T
    lane = lax.broadcasted_iota(jnp.int32, (HALO, LANES), 1)
    after = right[:, height : height + LANES]
    before = left[:, height : height + LANES]
    target[tiles, HALO:first, :] = jnp.where(
        lane < HALO, after, pltpu.roll(before, LANES - HALO, axis=1)
    )
    target[tiles, first + height : first + height + HALO, :] = jnp.where(
        lane < HALO, pltpu.roll(after, LANES - HALO, axis=1), pltpu.roll(before, LANES - 2 * HALO, axis=1)
    )


def spread_kernel(scale, x_ref, y_ref, above_ref, below_ref, left_ref, right_ref, out_ref):
    height, width = x_ref.shape
    for f, field_ref in enumerate((x_ref, y_ref)):
        for t in range(width // LANES):
            out_ref[f, t, 2 * HALO : 2 * HALO + height, :] = (
                field_ref[:, t * LANES : (t + 1) * LANES] * scale
            )
        fill_halo(
            out_ref.at[f], height, width, above_ref[f] * scale, below_ref[f] * scale,
            left_ref[f] * scale, right_ref[f] * scale,
        )


def edges_kernel(*refs):
    first_rows, last_rows, first_cols, last_cols = refs[8:]
    for f in range(2):
        top, bottom, left, right = refs[4 * f : 4 * f + 4]
        first_rows[f] = top[...]
        last_rows[f] = bottom[...]
        first_cols[f] = left[...].T[:HALO]
        last_cols[f] = right[...].T[-HALO:]


def edges(x, y):
    height, width = x.shape
    specs = [
        pl.BlockSpec((HALO, width), lambda i: (0, 0)),
        pl.BlockSpec((HALO, width), lambda i: (height // HALO - 1, 0)),
        pl.BlockSpec((height, LANES), lambda i: (0, 0)),
        pl.BlockSpec((height, LANES), lambda i: (0, width // LANES - 1)),
    ]
    shapes = [(2, HALO, width)] * 2 + [(2, HALO, height)] * 2
    return pl.pallas_call(
        edges_kernel,
        grid=(1,),
        out_shape=[jax.ShapeDtypeStruct(shape, jnp.float32) for shape in shapes],
        in_specs=specs * 2,
        out_specs=[pl.BlockSpec(shape, lambda i: (0, 0, 0)) for shape in shapes],
        name="velocity_edges",
    )(*[x] * 4, *[y] * 4)


def spread(x, y, above, below, left, right, scale):
    height, width = x.shape
    vmem = pl.BlockSpec(memory_space=pltpu.VMEM)
    return pl.pallas_call(
        functools.partial(spread_kernel, scale),
        out_shape=jax.ShapeDtypeStruct(
            (2, width // LANES + 1, height + 4 * HALO, LANES), jnp.float32
        ),
        in_specs=[vmem] * 6,
        out_specs=vmem,
        compiler_params=pltpu.CompilerParams(vmem_limit_bytes=VMEM_LIMIT),
        name="spread_velocity",
    )(x, y, above, below, left, right)


def steps_kernel(
    chunk, nodal_ref, velocity_ref, above_ref, below_ref, left_ref, right_ref, out_ref, field,
    middle, speed, sem,
):
    tiles, height, _ = nodal_ref.shape
    copies = [
        pltpu.make_async_copy(
            nodal_ref, field.at[pl.ds(0, tiles), pl.ds(2 * HALO, height), :], sem.at[0]
        ),
        pltpu.make_async_copy(velocity_ref, speed, sem.at[1]),
    ]
    for copy in copies:
        copy.start()
    fill_halo(
        field, height, tiles * LANES, above_ref[...], below_ref[...], left_ref[...], right_ref[...]
    )
    for copy in copies:
        copy.wait()
    lane = lax.broadcasted_iota(jnp.int32, (chunk, LANES), 1)
    count = tiles + 1
    scale = TIME_STEP * DIFFUSION / 12.0

    def advance(source, start, tile_range, store):
        rolled = {}

        def centre(t):
            return source[t, pl.ds(start, chunk), :]

        def turned(t, by):
            if (t, by) not in rolled:
                rolled[t, by] = pltpu.roll(centre(t), by % LANES, axis=1)
            return rolled[t, by]

        for t in tile_range:
            here = centre(t)
            up, down = (t + 1) % count, (t - 1) % count
            one_below = source[t, pl.ds(start - 1, chunk), :]
            one_above = source[t, pl.ds(start + 1, chunk), :]
            two_below = source[t, pl.ds(start - 2, chunk), :]
            two_above = source[t, pl.ds(start + 2, chunk), :]
            south_one = jnp.where(lane < 1, turned(down, 1), turned(t, 1))
            south_two = jnp.where(lane < 2, turned(down, 2), turned(t, 2))
            north_one = jnp.where(lane >= LANES - 1, turned(up, -1), turned(t, -1))
            north_two = jnp.where(lane >= LANES - 2, turned(up, -2), turned(t, -2))
            near = (one_above + one_below) + (north_one + south_one)
            far = (two_above + two_below) + (north_two + south_two)
            slope_x = 8.0 * (one_above - one_below) - (two_above - two_below)
            slope_y = 8.0 * (north_one - south_one) - (north_two - south_two)
            change = (16.0 * scale) * near - scale * far
            change = change - speed[0, t, pl.ds(start, chunk), :] * slope_x
            change = change - speed[1, t, pl.ds(start, chunk), :] * slope_y
            store(t, here, (1.0 - 60.0 * scale) * here + change)

    def first_half(c, carry):
        start = pl.multiple_of(HALO + c * chunk, HALO)

        def store(t, here, result):
            middle[t, pl.ds(start, chunk), :] = result

        advance(field, start, range(count), store)
        return carry

    def second_half(c, carry):
        start = pl.multiple_of(HALO + c * chunk, HALO)

        def store(t, here, result):
            field[t, pl.ds(start, chunk), :] = 0.5 * (field[t, pl.ds(start, chunk), :] + result)

        advance(middle, start, range(count), store)
        return carry

    def last_half(c, carry):
        start = pl.multiple_of(2 * HALO + c * chunk, HALO)
        place = pl.multiple_of(c * chunk, HALO)

        def store(t, here, result):
            out_ref[pl.ds(place, chunk), t * LANES : (t + 1) * LANES] = 0.5 * (
                field[t, pl.ds(start, chunk), :] + result
            )

        advance(middle, start, range(tiles), store)
        return carry

    extended = (height + 2 * HALO) // chunk
    for step in range(STEPS):
        lax.fori_loop(0, extended, first_half, 0)
        if step < STEPS - 1:
            lax.fori_loop(0, extended, second_half, 0)
    lax.fori_loop(0, height // chunk, last_half, 0)


def run_steps(nodal, velocity, above, below, left, right):
    tiles, height, _ = nodal.shape
    vmem = pl.BlockSpec(memory_space=pltpu.VMEM)
    anywhere = pl.BlockSpec(memory_space=pl.ANY)
    extended = (tiles + 1, height + 4 * HALO, LANES)
    return pl.pallas_call(
        functools.partial(steps_kernel, 2 * HALO),
        out_shape=jax.ShapeDtypeStruct((height, tiles * LANES), jnp.float32),
        in_specs=[anywhere, anywhere] + [vmem] * 4,
        out_specs=vmem,
        scratch_shapes=[
            pltpu.VMEM(extended, jnp.float32),
            pltpu.VMEM(extended, jnp.float32),
            pltpu.VMEM((2,) + extended, jnp.float32),
            pltpu.SemaphoreType.DMA((2,)),
        ],
        compiler_params=pltpu.CompilerParams(vmem_limit_bytes=VMEM_LIMIT),
        name="heun_steps",
    )(nodal, velocity, above, below, left, right)


def hat_matrix(size):
    place = lax.broadcasted_iota(jnp.int32, (size, size), 0)
    node = lax.broadcasted_iota(jnp.int32, (size, size), 1)
    return jnp.where(node == 0, 1.0 - place.astype(jnp.float32) / size, hat_value(node, place))


def hat_value(node, place):
    spacing = jnp.maximum(node & (-node), 1).astype(jnp.float32)
    return jnp.maximum(0.0, 1.0 - jnp.abs(place - node).astype(jnp.float32) / spacing)


def coarse_share(node, place):
    return jnp.where(node == 0, 1.0, hat_value(node, place))


def weight_pattern(grid_levels, coefficients, faulty_grids):
    grid_ids = jnp.arange(coefficients.shape[0], dtype=jnp.int32)
    alive = jnp.all(faulty_grids[None, :] != grid_ids[:, None], axis=1)
    share = jnp.where(alive, coefficients, 0).astype(jnp.float32)
    row = lax.broadcasted_iota(jnp.int32, (8, LANES), 0)[None]
    lane = lax.broadcasted_iota(jnp.int32, (8, LANES), 1)[None]
    mask_x = (jnp.int32(1) << grid_levels[:, 0]) - 1
    mask_y = (jnp.int32(1) << grid_levels[:, 1]) - 1
    covered = ((row & mask_x[:, None, None]) == 0) & ((lane & mask_y[:, None, None]) == 0)
    return jnp.sum(jnp.where(covered, share[:, None, None], 0.0), axis=0)


def ring(axis):
    size = lax.axis_size(axis)
    up = [(i, (i + 1) % size) for i in range(size)]
    return up, [(j, i) for i, j in up]


def swap_rows(first, last):
    up, down = ring("gx")
    return lax.ppermute(last, "gx", up), lax.ppermute(first, "gx", down)


def swap_columns(first, last, above, below):
    up, down = ring("gy")
    room = jnp.zeros(first.shape[:-1] + (LANES - 2 * HALO,), jnp.float32)
    send_up = jnp.concatenate([last, above[..., -HALO:], below[..., -HALO:], room], axis=-1)
    send_down = jnp.concatenate([first, above[..., :HALO], below[..., :HALO], room], axis=-1)
    return lax.ppermute(send_up, "gy", up), lax.ppermute(send_down, "gy", down)


def local(
    owned_surplus, tile_owner, grid_levels, coefficients, faulty_grids, velocity_x, velocity_y
):
    slot_count, tile_height, tile_width = owned_surplus.shape
    rows_local, cols_local = velocity_x.shape
    size_x = lax.axis_size("gx")
    size_y = lax.axis_size("gy")
    device_count = size_x * size_y
    capacity = 2 * slot_count // device_count
    tiles_down = rows_local // tile_height
    tiles_across = cols_local // tile_width
    index_x = lax.axis_index("gx")
    index_y = lax.axis_index("gy")
    own_index = index_x * size_y + index_y
    offsets = tile_owner[:slot_count]
    positions = jnp.arange(slot_count, dtype=jnp.int32)
    same_offset = offsets[:, None] == offsets[None, :]
    earlier = positions[None, :] < positions[:, None]
    slot_rank = jnp.sum((same_offset & earlier).astype(jnp.int32), axis=1)
    target = (own_index - offsets) % device_count
    source = (own_index + offsets) % device_count
    outgoing = pack(target * capacity + slot_rank, owned_surplus, capacity)
    incoming = lax.all_to_all(
        outgoing.reshape(device_count, capacity, tile_height, tile_width),
        ("gx", "gy"),
        split_axis=0,
        concat_axis=0,
        tiled=True,
    ).reshape(device_count * capacity, tile_height, tile_width)

    lead_rows = owned_surplus[:tiles_across, 0, :].reshape(-1, LANES)
    lead_cols = owned_surplus[::tiles_across, :, 0].reshape(-1, LANES)
    lead = jnp.concatenate([lead_rows, lead_cols], axis=0)[None]
    far = 4 if size_y % 4 == 0 else 1
    near = size_y // far
    owner_y = index_y[None]
    for count, stride in ((near, 1), (far, near)):
        parts = [lead]
        owners = [owner_y]
        for by in range(1, count):
            pairs = [
                (j, j + (((j // stride) + by) % count - (j // stride) % count) * stride)
                for j in range(size_y)
            ]
            parts.append(lax.ppermute(lead, "gy", pairs))
            digit = owner_y // stride % count
            owners.append(owner_y + ((digit - by) % count - digit) * stride)
        lead = jnp.concatenate(parts, axis=0)
        owner_y = jnp.concatenate(owners)
    lead = lead.reshape(size_y, -1)
    lead_rows = lead[:, :cols_local]
    lead_cols = lead[:, cols_local:]
    owner = (index_x * size_y + owner_y)[:, None]
    offset_rows = jnp.repeat(offsets[:tiles_across], tile_width)
    offset_cols = jnp.repeat(offsets[::tiles_across], tile_height)
    row_block = (owner - offset_rows[None]) % device_count
    col_block = (owner - offset_cols[None]) % device_count
    corner_block = (owner - offsets[0]) % device_count
    places_y = (index_y, index_y + 1)
    own_piece = jnp.sum(jnp.where(row_block % size_y == index_y, lead_rows, 0.0), axis=0)
    own_piece = own_piece.reshape(-1, LANES)

    def share_for(peer):
        cols = [
            jnp.sum(
                jnp.where(col_block // size_y == peer, coarse_share(col_block % size_y, place), 0.0)
                * lead_cols,
                axis=0,
            ).reshape(-1, LANES)
            for place in places_y
        ]
        corners = [
            jnp.sum(
                coarse_share(corner_block // size_y, x)
                * coarse_share(corner_block % size_y, y)
                * lead_rows[:, :1]
            )
            for x in (peer, peer + 1)
            for y in places_y
        ]
        corners = jnp.repeat(jnp.stack(corners), LANES // 4).reshape(1, LANES)
        return jnp.concatenate([own_piece] + cols + [corners], axis=0)

    received = []
    for by in range(size_x):
        share = share_for((index_x + by) % size_x)
        if by:
            pairs = [(i, (i + by) % size_x) for i in range(size_x)]
            share = lax.ppermute(share, "gx", pairs)
        received.append(share)
    received = jnp.stack(received)
    weight = weight_pattern(grid_levels, coefficients, faulty_grids)
    row_count = cols_local // LANES
    pieces = received[:, :row_count].reshape(size_x, cols_local)
    total = jnp.sum(received[:, row_count:], axis=0)
    cols = total[:-1].reshape(2, rows_local)
    corners = total[-1, :: LANES // 4].reshape(2, 2) * weight[0, 0]
    sender = (index_x - jnp.arange(size_x, dtype=jnp.int32)) % size_x
    piece_owner = sender[:, None] * size_y + (index_y + offset_rows[None]) % size_y
    piece_block = (piece_owner - offset_rows[None]) % device_count // size_y
    row_weight = jnp.tile(weight[0], cols_local // LANES)
    rows = [
        jnp.sum(coarse_share(piece_block, place) * pieces, axis=0) * row_weight
        for place in (index_x, index_x + 1)
    ]
    col_weight = jnp.tile(weight[:, 0], rows_local // 8)
    local_row = jnp.arange(rows_local, dtype=jnp.int32)
    hat_rows = hat_matrix(rows_local)
    ramp = local_row.astype(jnp.float32) / rows_local
    first = jnp.where(local_row == 0, corners[0][:, None], cols * col_weight)
    lead_nodal = (
        jnp.dot(hat_rows, first.T, precision=lax.Precision.HIGHEST) + ramp[:, None] * corners[1][None]
    )
    hat = hat_matrix(HAT).astype(jnp.bfloat16)

    first_rows, last_rows, first_cols, last_cols = edges(velocity_x, velocity_y)
    above, below = swap_rows(first_rows, last_rows)
    left, right = swap_columns(first_cols, last_cols, above, below)
    speed = spread(velocity_x, velocity_y, above, below, left, right, TIME_STEP / 12.0)

    nodal, first_cols, last_cols = refine_block(
        source * capacity + slot_rank, incoming, weight, hat, hat.T, jnp.stack(rows), lead_nodal,
        rows_local, cols_local,
    )
    flat = lambda strip: strip.transpose(1, 0, 2).reshape(HALO, cols_local)
    above, below = swap_rows(flat(nodal[:, :HALO]), flat(nodal[:, -HALO:]))
    left, right = swap_columns(first_cols, last_cols, above, below)
    return run_steps(nodal, speed, above, below, left, right)


def solution(mesh):
    return jax.shard_map(
        local,
        mesh=mesh,
        in_specs=(P(("gx", "gy"), None, None), P(), P(), P(), P(), P("gx", "gy"), P("gx", "gy")),
        out_specs=P("gx", "gy"),
        check_vma=False,
    )
```

```python
import functools

import jax
import jax.numpy as jnp
from jax import lax
from jax.experimental import pallas as pl
from jax.experimental.pallas import tpu as pltpu
from jax.sharding import PartitionSpec as P

STEPS = 2
TIME_STEP = 0.2
DIFFUSION = 0.5
HALO = 8
LANES = 128
HAT = 256
VMEM_LIMIT = 48 << 20


def pack_kernel(tiles_across, capacity, target_ref, rank_ref, owned_ref, outgoing_ref):
    count, tile_rows, _ = owned_ref.shape
    messages = outgoing_ref.shape[0]
    half = tile_rows
    rows = []
    for ky in range(tiles_across):
        rows += [owned_ref[ky, 0:1, :LANES], owned_ref[ky, 0:1, LANES:]]
    per_part = LANES // tile_rows
    for part in range(count // tiles_across // per_part):
        columns = [
            owned_ref[(part * per_part + t) * tiles_across, :, :LANES] for t in range(per_part)
        ]
        rows.append(jnp.concatenate(columns, axis=0).T[0:1])
    rows += [rows[0]] * 4
    lead = jnp.concatenate(rows, axis=0)

    def address(m, carry):
        outgoing_ref[m, pl.ds(2 * half * capacity, lead.shape[0]), :] = lead
        return carry

    lax.fori_loop(0, messages, address, 0, unroll=8)

    def place(k, carry):
        m = target_ref[k]
        row = pl.multiple_of(rank_ref[k] * (2 * half), 2 * half)
        outgoing_ref[m, pl.ds(row, half), :] = owned_ref[k, :, :LANES]
        outgoing_ref[m, pl.ds(row + half, half), :] = owned_ref[k, :, LANES:]
        return carry

    lax.fori_loop(0, count, place, 0, unroll=8)


def pack(target, rank, owned, messages, capacity, tiles_across):
    count, tile_rows, _ = owned.shape
    lead_rows = 2 * tiles_across + count // tiles_across * tile_rows // LANES + 4
    smem = pl.BlockSpec(memory_space=pltpu.SMEM)
    vmem = pl.BlockSpec(memory_space=pltpu.VMEM)
    return pl.pallas_call(
        functools.partial(pack_kernel, tiles_across, capacity),
        out_shape=jax.ShapeDtypeStruct(
            (messages, capacity * tile_rows * 2 + lead_rows, LANES), owned.dtype
        ),
        in_specs=[smem, smem, vmem],
        out_specs=vmem,
        compiler_params=pltpu.CompilerParams(vmem_limit_bytes=VMEM_LIMIT),
        name="pack_tiles",
    )(target, rank, owned)


def split_dot(left, right, split_left):
    value = left if split_left else right
    high = value.astype(jnp.bfloat16)
    low = (value - high.astype(jnp.float32)).astype(jnp.bfloat16)
    if split_left:
        pairs = ((high, right), (low, right))
    else:
        pairs = ((left, high), (left, low))
    return sum(jnp.dot(a, b, preferred_element_type=jnp.float32) for a, b in pairs)


def refine_kernel(
    tiles_across, tile_rows, capacity, source_ref, rank_ref, incoming_ref, share_ref, weight_ref,
    hat_x_ref, hat_y_ref, nodal_ref, first_rows_ref, last_rows_ref, left_ref, right_ref,
    block, edge,
):
    height = nodal_ref.shape[1]
    tiles_down = height // tile_rows
    row_parts = 2 * tiles_across
    col_parts = height // LANES
    lead_row = 2 * tile_rows * capacity
    lead_size = share_ref.shape[2]
    tile_weight = jnp.concatenate([weight_ref[...]] * (tile_rows // 8), axis=0)

    def place(kx, carry):
        row = pl.multiple_of(kx * tile_rows, tile_rows)
        for ky in range(tiles_across):
            message = source_ref[kx * tiles_across + ky]
            start = pl.multiple_of(rank_ref[kx * tiles_across + ky] * (2 * tile_rows), 2 * tile_rows)
            for part in range(2):
                block[pl.ds(row, tile_rows), (2 * ky + part) * LANES : (2 * ky + part + 1) * LANES] = (
                    incoming_ref[message, pl.ds(start + part * tile_rows, tile_rows), :] * tile_weight
                )
        return carry

    lax.fori_loop(0, tiles_down, place, 0, unroll=2)

    def collect(m, sums):
        lead = incoming_ref[m, pl.ds(lead_row, lead_size), :]
        return tuple(total + share_ref[i, m] * lead for i, total in enumerate(sums))

    zero = jnp.zeros((lead_size, LANES), jnp.float32)
    own_lead, next_lead = lax.fori_loop(0, incoming_ref.shape[0], collect, (zero, zero), unroll=8)

    weight = weight_ref[...]
    lane = lax.broadcasted_iota(jnp.int32, (1, LANES), 1)
    corner_base = row_parts + col_parts
    corner = lambda x: weight[0:1, 0:1] * jnp.where(
        lane == 0,
        own_lead[corner_base + 2 * x : corner_base + 2 * x + 1, 0:1],
        own_lead[corner_base + 2 * x + 1 : corner_base + 2 * x + 2, 0:1],
    )
    for part in range(col_parts):
        pair = jnp.concatenate(
            [
                own_lead[row_parts + part : row_parts + part + 1],
                next_lead[row_parts + part : row_parts + part + 1],
                jnp.zeros((LANES - 2, LANES), jnp.float32),
            ],
            axis=0,
        ).T
        edge[part * LANES : (part + 1) * LANES, :] = (
            pair.reshape(LANES // 8, 8, LANES) * weight[:, 0:1][None]
        ).reshape(LANES, LANES)

    row_id = lax.broadcasted_iota(jnp.int32, (HAT, HAT), 0)
    lane_id = lax.broadcasted_iota(jnp.int32, (HAT, HAT), 1)
    ramp_rows = row_id.astype(jnp.float32) * (1.0 / HAT)
    ramp_lanes = lane_id.astype(jnp.float32) * (1.0 / HAT)

    def refine_down(target, lanes, own, after):
        width = own.shape[1]
        middle = target[HAT : HAT + 1, lanes] + 0.5 * (own + after)
        for part, (first, last) in enumerate(((own, middle), (middle, after))):
            rows = slice(part * HAT, (part + 1) * HAT)
            values = jnp.where(row_id[:, :width] == 0, first, target[rows, lanes])
            target[rows, lanes] = split_dot(hat_x_ref[...], values, False) + ramp_rows[:, :width] * last

    refine_down(edge, slice(0, LANES), corner(0), corner(1))
    line = lambda lead, ky: (
        jnp.concatenate([lead[2 * ky : 2 * ky + 1], lead[2 * ky + 1 : 2 * ky + 2]], axis=1)
        * jnp.concatenate([weight[0:1]] * 2, axis=1)
    )
    for ky in range(tiles_across):
        refine_down(
            block, slice(ky * HAT, (ky + 1) * HAT), line(own_lead, ky), line(next_lead, ky)
        )
    for part in range(height // HAT):
        rows = slice(part * HAT, (part + 1) * HAT)
        ends = [edge[rows, 0:1], None, None, None, edge[rows, 1:2]]
        for middle, before, after in ((2, 0, 4), (1, 0, 2), (3, 2, 4)):
            ends[middle] = block[rows, middle * HAT : middle * HAT + 1] + 0.5 * (
                ends[before] + ends[after]
            )
        for ky in range(tiles_across):
            values = jnp.where(lane_id == 0, ends[ky], block[rows, ky * HAT : (ky + 1) * HAT])
            result = split_dot(values, hat_y_ref[...], True) + ramp_lanes * ends[ky + 1]
            nodal_ref[2 * ky, rows, :] = result[:, :LANES]
            nodal_ref[2 * ky + 1, rows, :] = result[:, LANES:]
            columns = slice(ky * HAT, (ky + 1) * HAT)
            if part == 0:
                first_rows_ref[:, columns] = result[:HALO]
            if part == height // HAT - 1:
                last_rows_ref[:, columns] = result[-HALO:]
            if ky == 0:
                left_ref[:, rows] = result[:, :LANES].T[:HALO]
            if ky == tiles_across - 1:
                right_ref[:, rows] = result[:, LANES:].T[-HALO:]


def refine_block(source, rank, incoming, share, weight, hat_x, hat_y, height, width, tile_rows, capacity):
    vmem = pl.BlockSpec(memory_space=pltpu.VMEM)
    smem = pl.BlockSpec(memory_space=pltpu.SMEM)
    shapes = [(width // LANES, height, LANES)] + [(HALO, width)] * 2 + [(HALO, height)] * 2
    return pl.pallas_call(
        functools.partial(refine_kernel, width // HAT, tile_rows, capacity),
        out_shape=[jax.ShapeDtypeStruct(shape, jnp.float32) for shape in shapes],
        in_specs=[smem, smem] + [vmem] * 5,
        out_specs=[vmem] * len(shapes),
        scratch_shapes=[
            pltpu.VMEM((height, width), jnp.float32), pltpu.VMEM((height, LANES), jnp.float32)
        ],
        compiler_params=pltpu.CompilerParams(vmem_limit_bytes=VMEM_LIMIT),
        name="refine_block",
    )(source, rank, incoming, share, weight, hat_x, hat_y)


def fill_halo(target, height, width, above, below, left, right, above_side, below_side):
    tiles = width // LANES
    first = 2 * HALO
    end = first + height
    for t in range(tiles):
        target[t, HALO:first, :] = above[:, t * LANES : (t + 1) * LANES]
        target[t, end : end + HALO, :] = below[:, t * LANES : (t + 1) * LANES]
    between = jnp.zeros((LANES - 2 * HALO, height), jnp.float32)
    target[tiles, first:end, :] = jnp.concatenate([right, between, left], axis=0).T
    target[tiles, HALO:first, :] = above_side
    target[tiles, end : end + HALO, :] = below_side


def edges_kernel(*refs):
    first_rows, last_rows, first_cols, last_cols = refs[8:]
    for f in range(2):
        top, bottom, left, right = refs[4 * f : 4 * f + 4]
        first_rows[f] = top[...]
        last_rows[f] = bottom[...]
        first_cols[f] = left[...].T[:HALO]
        last_cols[f] = right[...].T[-HALO:]


def edges(x, y):
    height, width = x.shape
    specs = [
        pl.BlockSpec((HALO, width), lambda i: (0, 0)),
        pl.BlockSpec((HALO, width), lambda i: (height // HALO - 1, 0)),
        pl.BlockSpec((height, LANES), lambda i: (0, 0)),
        pl.BlockSpec((height, LANES), lambda i: (0, width // LANES - 1)),
    ]
    shapes = [(2, HALO, width)] * 2 + [(2, HALO, height)] * 2
    return pl.pallas_call(
        edges_kernel,
        grid=(1,),
        out_shape=[jax.ShapeDtypeStruct(shape, jnp.float32) for shape in shapes],
        in_specs=specs * 2,
        out_specs=[pl.BlockSpec(shape, lambda i: (0, 0, 0)) for shape in shapes],
        name="velocity_edges",
    )(*[x] * 4, *[y] * 4)


def steps_kernel(
    chunk, last_chunk, nodal_ref, x_ref, y_ref, stencil_ref, rows_above, rows_below, speed_above,
    speed_below, speed_left, speed_right, from_left, from_right, out_ref, field, middle, speed,
):
    tiles, height, _ = nodal_ref.shape
    width = tiles * LANES
    count = tiles + 1
    scale = TIME_STEP * DIFFUSION / 12.0
    speed_scale = TIME_STEP / 12.0
    side = lax.broadcasted_iota(jnp.int32, (HALO, LANES), 1)

    def corner(k):
        part = slice(height + k * LANES, height + (k + 1) * LANES)
        return jnp.where(side < LANES // 2, from_right[:, part], from_left[:, part])

    for t in range(tiles):
        field[t, 2 * HALO : 2 * HALO + height, :] = nodal_ref[t]
    fill_halo(
        field, height, width, rows_above, rows_below, from_left[:, :height], from_right[:, :height],
        corner(0), corner(1),
    )
    for f, velocity in enumerate((x_ref, y_ref)):
        for t in range(tiles):
            speed[f, t, 2 * HALO : 2 * HALO + height, :] = (
                velocity[:, t * LANES : (t + 1) * LANES] * speed_scale
            )
        fill_halo(
            speed.at[f], height, width, speed_above[f] * speed_scale, speed_below[f] * speed_scale,
            speed_left[f] * speed_scale, speed_right[f] * speed_scale,
            corner(2 + 2 * f) * speed_scale, corner(3 + 2 * f) * speed_scale,
        )

    def advance(source, start, size, tile_range, store):
        parts = {}
        lane = lax.broadcasted_iota(jnp.int32, (size, LANES), 1)

        def split(t):
            if t not in parts:
                value = source[t, pl.ds(start, size), :]
                high = value.astype(jnp.bfloat16)
                parts[t] = (high, (value - high.astype(jnp.float32)).astype(jnp.bfloat16))
            return parts[t]

        for t in tile_range:
            before, after = split((t - 1) % count), split((t + 1) % count)
            around = [jnp.where(lane >= LANES // 2, b, a) for b, a in zip(before, after)]
            across = jnp.dot(
                jnp.concatenate([*split(t), *around], axis=1),
                stencil_ref[...],
                preferred_element_type=jnp.float32,
            )
            here = source[t, pl.ds(start, size), :]
            one_below = source[t, pl.ds(start - 1, size), :]
            one_above = source[t, pl.ds(start + 1, size), :]
            two_below = source[t, pl.ds(start - 2, size), :]
            two_above = source[t, pl.ds(start + 2, size), :]
            curve = 16.0 * (one_above + one_below) - (two_above + two_below) + across[:, :LANES]
            slope = 8.0 * (one_above - one_below) - (two_above - two_below)
            change = scale * curve - speed[0, t, pl.ds(start, size), :] * slope
            change = change - speed[1, t, pl.ds(start, size), :] * across[:, LANES:]
            store(t, (1.0 - 60.0 * scale) * here + change)

    def first_half(c, carry):
        start = pl.multiple_of(HALO + c * chunk, HALO)

        def store(t, result):
            middle[t, pl.ds(start, chunk), :] = result

        advance(field, start, chunk, range(count), store)
        return carry

    def second_half(c, carry):
        start = pl.multiple_of(HALO + c * chunk, HALO)

        def store(t, result):
            field[t, pl.ds(start, chunk), :] = 0.5 * (field[t, pl.ds(start, chunk), :] + result)

        advance(middle, start, chunk, range(count), store)
        return carry

    def last_half(c, carry):
        start = pl.multiple_of(2 * HALO + c * last_chunk, HALO)
        place = pl.multiple_of(c * last_chunk, HALO)

        def store(t, result):
            out_ref[pl.ds(place, last_chunk), t * LANES : (t + 1) * LANES] = 0.5 * (
                field[t, pl.ds(start, last_chunk), :] + result
            )

        advance(middle, start, last_chunk, range(tiles), store)
        return carry

    extended = (height + 2 * HALO) // chunk
    for step in range(STEPS):
        lax.fori_loop(0, extended, first_half, 0)
        if step < STEPS - 1:
            lax.fori_loop(0, extended, second_half, 0)
    lax.fori_loop(0, height // last_chunk, last_half, 0)


def largest_chunk(rows, limit):
    return max(size for size in range(16, limit + 1, 16) if rows % size == 0)


def run_steps(nodal, x, y, stencil, *halo):
    tiles, height, _ = nodal.shape
    vmem = pl.BlockSpec(memory_space=pltpu.VMEM)
    extended = (tiles + 1, height + 4 * HALO, LANES)
    return pl.pallas_call(
        functools.partial(
            steps_kernel, largest_chunk(height + 2 * HALO, 192), largest_chunk(height, 192)
        ),
        out_shape=jax.ShapeDtypeStruct((height, tiles * LANES), jnp.float32),
        in_specs=[vmem] * (4 + len(halo)),
        out_specs=vmem,
        scratch_shapes=[
            pltpu.VMEM(extended, jnp.float32),
            pltpu.VMEM(extended, jnp.float32),
            pltpu.VMEM((2,) + extended, jnp.float32),
        ],
        compiler_params=pltpu.CompilerParams(vmem_limit_bytes=VMEM_LIMIT),
        name="heun_steps",
    )(nodal, x, y, stencil, *halo)


def stencil_matrix():
    row = lax.broadcasted_iota(jnp.int32, (4 * LANES, 2 * LANES), 0)
    column = lax.broadcasted_iota(jnp.int32, (4 * LANES, 2 * LANES), 1)
    lane = row % LANES
    outside = jnp.where(lane < LANES // 2, lane + LANES, lane - LANES)
    shift = jnp.where(row < 2 * LANES, lane, outside) - column % LANES
    distance = jnp.abs(shift)
    curve = jnp.where(distance == 1, 16.0, jnp.where(distance == 2, -1.0, 0.0))
    slope = jnp.where(distance == 1, 8.0, jnp.where(distance == 2, -1.0, 0.0)) * jnp.sign(
        shift
    ).astype(jnp.float32)
    return jnp.where(column < LANES, curve, slope).astype(jnp.bfloat16)


def hat_matrix(size):
    place = lax.broadcasted_iota(jnp.int32, (size, size), 0)
    node = lax.broadcasted_iota(jnp.int32, (size, size), 1)
    return jnp.where(node == 0, 1.0 - place.astype(jnp.float32) / size, hat_value(node, place))


def hat_value(node, place):
    spacing = jnp.maximum(node & (-node), 1).astype(jnp.float32)
    return jnp.maximum(0.0, 1.0 - jnp.abs(place - node).astype(jnp.float32) / spacing)


def coarse_share(node, place):
    return jnp.where(node == 0, 1.0, hat_value(node, place))


def weight_pattern(grid_levels, coefficients, faulty_grids):
    grid_ids = jnp.arange(coefficients.shape[0], dtype=jnp.int32)
    alive = jnp.all(faulty_grids[None, :] != grid_ids[:, None], axis=1)
    share = jnp.where(alive, coefficients, 0).astype(jnp.float32)
    row = lax.broadcasted_iota(jnp.int32, (8, LANES), 0)[None]
    lane = lax.broadcasted_iota(jnp.int32, (8, LANES), 1)[None]
    mask_x = (jnp.int32(1) << grid_levels[:, 0]) - 1
    mask_y = (jnp.int32(1) << grid_levels[:, 1]) - 1
    covered = ((row & mask_x[:, None, None]) == 0) & ((lane & mask_y[:, None, None]) == 0)
    return jnp.sum(jnp.where(covered, share[:, None, None], 0.0), axis=0)


def shifted(array, axis, by):
    size = lax.axis_size(axis)
    return lax.ppermute(array, axis, [(i, (i + by) % size) for i in range(size)])


def lead_share(offsets, index_x, index_y, size_x, size_y, tiles_across, tile_height):
    devices = size_x * size_y
    row_parts = 2 * tiles_across
    by_row = jnp.repeat(offsets[:tiles_across], 2)[:, None]
    by_col = jnp.repeat(offsets[::tiles_across], tile_height).reshape(-1, LANES)
    spread_row = jnp.broadcast_to(by_row, (row_parts, LANES))
    spread_corner = jnp.broadcast_to(offsets[0], (4, LANES))
    table = jnp.concatenate([spread_row, by_col, spread_corner], axis=0)
    owner = lax.broadcasted_iota(jnp.int32, (devices, 1, 1), 0)
    block = (owner - table[None]) % devices
    x, y = block // size_y, block % size_y
    line = lax.broadcasted_iota(jnp.int32, (1, table.shape[0], 1), 1)
    corner = line - (table.shape[0] - 4)
    shares = []
    for by in range(2):
        rows = jnp.where(y == index_y, coarse_share(x, index_x + by), 0.0)
        cols = jnp.where(x == index_x, coarse_share(y, index_y + by), 0.0)
        corners = coarse_share(x, index_x + corner // 2) * coarse_share(y, index_y + corner % 2)
        shares.append(
            jnp.where(line < row_parts, rows, jnp.where(corner < 0, cols, corners))
        )
    return jnp.stack(shares)


def local(
    owned_surplus, tile_owner, grid_levels, coefficients, faulty_grids, velocity_x, velocity_y
):
    slot_count, tile_height, tile_width = owned_surplus.shape
    rows_local, cols_local = velocity_x.shape
    size_x = lax.axis_size("gx")
    size_y = lax.axis_size("gy")
    device_count = size_x * size_y
    capacity = 2 * slot_count // device_count
    tiles_across = cols_local // tile_width
    index_x = lax.axis_index("gx")
    index_y = lax.axis_index("gy")
    own_index = index_x * size_y + index_y
    offsets = tile_owner[:slot_count]
    positions = jnp.arange(slot_count, dtype=jnp.int32)
    same_offset = offsets[:, None] == offsets[None, :]
    earlier = positions[None, :] < positions[:, None]
    slot_rank = jnp.sum((same_offset & earlier).astype(jnp.int32), axis=1)
    target = (own_index - offsets) % device_count
    source = (own_index + offsets) % device_count
    outgoing = pack(target, slot_rank, owned_surplus, device_count, capacity, tiles_across)
    incoming = lax.all_to_all(outgoing, ("gx", "gy"), split_axis=0, concat_axis=0, tiled=True)

    first_rows, last_rows, first_cols, last_cols = edges(velocity_x, velocity_y)
    speed_halo = (
        shifted(last_rows, "gx", 1),
        shifted(first_rows, "gx", -1),
        shifted(last_cols, "gy", 1),
        shifted(first_cols, "gy", -1),
    )
    incoming, speed_halo = lax.optimization_barrier((incoming, speed_halo))
    share = lead_share(offsets, index_x, index_y, size_x, size_y, tiles_across, tile_height)
    weight = weight_pattern(grid_levels, coefficients, faulty_grids)
    hat = hat_matrix(HAT).astype(jnp.bfloat16)

    nodal, first_rows, last_rows, first_cols, last_cols = refine_block(
        source, slot_rank, incoming, share, weight, hat, hat.T, rows_local, cols_local, tile_height,
        capacity,
    )
    above = shifted(last_rows, "gx", 1)
    below = shifted(first_rows, "gx", -1)
    strips = [above, below] + [side[f] for f in range(2) for side in speed_halo[:2]]
    from_left = shifted(
        jnp.concatenate([last_cols] + [strip[:, -LANES:] for strip in strips], axis=1), "gy", 1
    )
    from_right = shifted(
        jnp.concatenate([first_cols] + [strip[:, :LANES] for strip in strips], axis=1), "gy", -1
    )
    return run_steps(
        nodal, velocity_x, velocity_y, stencil_matrix(), above, below, *speed_halo, from_left, from_right
    )


def solution(mesh):
    return jax.shard_map(
        local,
        mesh=mesh,
        in_specs=(P(("gx", "gy"), None, None), P(), P(), P(), P(), P("gx", "gy"), P("gx", "gy")),
        out_specs=P("gx", "gy"),
        check_vma=False,
    )
```

```python
import functools

import jax
import jax.numpy as jnp
from jax import lax
from jax.experimental import pallas as pl
from jax.experimental.pallas import tpu as pltpu
from jax.sharding import PartitionSpec as P

STEPS = 2
TIME_STEP = 0.2
DIFFUSION = 0.5
HALO = 8
LANES = 128
HAT = 256
VMEM_LIMIT = 48 << 20
PACK_LIMIT = 60 << 20


def pack_kernel(
    tiles_across, capacity, owner_ref, owned_ref, outgoing_ref, staged, wide, leads, offsets, used,
    sem_in, sem_out, sem_lead, sem_owner,
):
    count, tile_rows, _ = owned_ref.shape
    messages = outgoing_ref.shape[0]
    size = 2 * tile_rows
    groups = sem_in.shape[0]
    per_group = count // groups

    def arrival(g):
        part = pl.ds(g * per_group, per_group)
        return pltpu.make_async_copy(owned_ref.at[part], staged.at[part], sem_in.at[g])

    head = pltpu.make_async_copy(owner_ref.at[pl.ds(0, count)], offsets, sem_owner)
    head.start()
    for g in range(groups):
        arrival(g).start()
    own_index = lax.axis_index("gx") * lax.axis_size("gy") + lax.axis_index("gy")

    def clear(m, carry):
        used[m] = 0
        return carry

    lax.fori_loop(0, messages, clear, 0, unroll=8)
    head.wait()
    for g in range(groups):
        arrival(g).wait()

        def place(i, carry, g=g):
            k = g * per_group + i
            wide[k, :tile_rows, :] = staged[k, :, :LANES]
            wide[k, tile_rows:, :] = staged[k, :, LANES:]
            offset = offsets[k]
            rank = used[offset]
            used[offset] = rank + 1
            target = lax.rem(own_index - offset + messages, messages)
            row = pl.multiple_of(rank * size, size)
            pltpu.make_async_copy(
                wide.at[k], outgoing_ref.at[target, pl.ds(row, size), :], sem_out
            ).start()
            return carry

        lax.fori_loop(0, per_group, place, 0, unroll=8)

    rows = []
    for ky in range(tiles_across):
        rows += [staged[ky, 0:1, :LANES], staged[ky, 0:1, LANES:]]
    per_part = LANES // tile_rows
    for part in range(count // tiles_across // per_part):
        columns = [staged[(part * per_part + t) * tiles_across, :, :LANES] for t in range(per_part)]
        rows.append(jnp.concatenate(columns, axis=0).T[0:1])
    rows += [rows[0]] * 4
    lead = jnp.concatenate(rows, axis=0)

    def address(m, carry):
        leads[m] = lead
        return carry

    lax.fori_loop(0, messages, address, 0, unroll=8)
    to_all = pltpu.make_async_copy(
        leads, outgoing_ref.at[:, pl.ds(size * capacity, lead.shape[0]), :], sem_lead
    )
    to_all.start()
    to_all.wait()
    pltpu.make_async_copy(wide, wide, sem_out).wait()


def pack(tile_owner, owned, messages, capacity, tiles_across):
    count, tile_rows, _ = owned.shape
    lead_rows = 2 * tiles_across + count // tiles_across * tile_rows // LANES + 4
    anywhere = pl.BlockSpec(memory_space=pl.ANY)
    return pl.pallas_call(
        functools.partial(pack_kernel, tiles_across, capacity),
        out_shape=jax.ShapeDtypeStruct(
            (messages, capacity * tile_rows * 2 + lead_rows, LANES), owned.dtype
        ),
        in_specs=[anywhere, anywhere],
        out_specs=anywhere,
        scratch_shapes=[
            pltpu.VMEM(owned.shape, owned.dtype),
            pltpu.VMEM((count, 2 * tile_rows, LANES), owned.dtype),
            pltpu.VMEM((messages, lead_rows, LANES), owned.dtype),
            pltpu.SMEM((count,), jnp.int32),
            pltpu.SMEM((messages,), jnp.int32),
            pltpu.SemaphoreType.DMA((8,)),
            pltpu.SemaphoreType.DMA,
            pltpu.SemaphoreType.DMA,
            pltpu.SemaphoreType.DMA,
        ],
        compiler_params=pltpu.CompilerParams(vmem_limit_bytes=PACK_LIMIT),
        name="pack_tiles",
    )(tile_owner, owned)


def split_dot(left, right, split_left):
    value = left if split_left else right
    high = value.astype(jnp.bfloat16)
    low = (value - high.astype(jnp.float32)).astype(jnp.bfloat16)
    if split_left:
        pairs = ((high, right), (low, right))
    else:
        pairs = ((left, high), (left, low))
    return sum(jnp.dot(a, b, preferred_element_type=jnp.float32) for a, b in pairs)


def refine_kernel(
    tiles_across, tile_rows, capacity, source_ref, rank_ref, incoming_ref, share_ref, weight_ref,
    hat_x_ref, hat_y_ref, nodal_ref, first_rows_ref, last_rows_ref, left_ref, right_ref,
    block, edge, staged, leads, sem_tile, sem_lead,
):
    height = nodal_ref.shape[1]
    tiles_down = height // tile_rows
    row_parts = 2 * tiles_across
    col_parts = height // LANES
    lead_row = 2 * tile_rows * capacity
    lead_size = share_ref.shape[2]
    tile_weight = jnp.concatenate([weight_ref[...]] * (tile_rows // 8), axis=0)
    size = 2 * tile_rows
    groups = sem_tile.shape[0]
    per_group = tiles_down * tiles_across // groups
    lead_copy = pltpu.make_async_copy(
        incoming_ref.at[:, pl.ds(lead_row, lead_size), :], leads, sem_lead
    )
    lead_copy.start()
    for g in range(groups):

        def fetch(i, carry, g=g):
            k = g * per_group + i
            row = pl.multiple_of(rank_ref[k] * size, size)
            pltpu.make_async_copy(
                incoming_ref.at[source_ref[k], pl.ds(row, size), :], staged.at[k], sem_tile.at[g]
            ).start()
            return carry

        lax.fori_loop(0, per_group, fetch, 0, unroll=8)
    lead_copy.wait()

    def collect(m, sums):
        lead = leads[m]
        return tuple(total + share_ref[i, m] * lead for i, total in enumerate(sums))

    zero = jnp.zeros((lead_size, LANES), jnp.float32)
    own_lead, next_lead = lax.fori_loop(0, leads.shape[0], collect, (zero, zero), unroll=8)

    weight = weight_ref[...]
    lane = lax.broadcasted_iota(jnp.int32, (1, LANES), 1)
    corner_base = row_parts + col_parts
    corner = lambda x: weight[0:1, 0:1] * jnp.where(
        lane == 0,
        own_lead[corner_base + 2 * x : corner_base + 2 * x + 1, 0:1],
        own_lead[corner_base + 2 * x + 1 : corner_base + 2 * x + 2, 0:1],
    )
    for part in range(col_parts):
        pair = jnp.concatenate(
            [
                own_lead[row_parts + part : row_parts + part + 1],
                next_lead[row_parts + part : row_parts + part + 1],
                jnp.zeros((LANES - 2, LANES), jnp.float32),
            ],
            axis=0,
        ).T
        edge[part * LANES : (part + 1) * LANES, :] = (
            pair.reshape(LANES // 8, 8, LANES) * weight[:, 0:1][None]
        ).reshape(LANES, LANES)

    row_id = lax.broadcasted_iota(jnp.int32, (HAT, HAT), 0)
    lane_id = lax.broadcasted_iota(jnp.int32, (HAT, HAT), 1)
    ramp_rows = row_id.astype(jnp.float32) * (1.0 / HAT)
    ramp_lanes = lane_id.astype(jnp.float32) * (1.0 / HAT)

    def refine_down(target, lanes, own, after):
        width = own.shape[1]
        middle = target[HAT : HAT + 1, lanes] + 0.5 * (own + after)
        for part, (first, last) in enumerate(((own, middle), (middle, after))):
            rows = slice(part * HAT, (part + 1) * HAT)
            values = jnp.where(row_id[:, :width] == 0, first, target[rows, lanes])
            target[rows, lanes] = split_dot(hat_x_ref[...], values, False) + ramp_rows[:, :width] * last

    refine_down(edge, slice(0, LANES), corner(0), corner(1))

    def place(kx, carry):
        row = pl.multiple_of(kx * tile_rows, tile_rows)
        for ky in range(tiles_across):
            for part in range(2):
                block[pl.ds(row, tile_rows), (2 * ky + part) * LANES : (2 * ky + part + 1) * LANES] = (
                    staged[kx * tiles_across + ky, part * tile_rows : (part + 1) * tile_rows, :]
                    * tile_weight
                )
        return carry

    for g in range(groups):
        part = staged.at[pl.ds(g * per_group, per_group)]
        pltpu.make_async_copy(part, part, sem_tile.at[g]).wait()
        lax.fori_loop(
            g * tiles_down // groups, (g + 1) * tiles_down // groups, place, 0, unroll=2
        )
    line = lambda lead, ky: (
        jnp.concatenate([lead[2 * ky : 2 * ky + 1], lead[2 * ky + 1 : 2 * ky + 2]], axis=1)
        * jnp.concatenate([weight[0:1]] * 2, axis=1)
    )
    for ky in range(tiles_across):
        refine_down(
            block, slice(ky * HAT, (ky + 1) * HAT), line(own_lead, ky), line(next_lead, ky)
        )
    for part in range(height // HAT):
        rows = slice(part * HAT, (part + 1) * HAT)
        ends = [edge[rows, 0:1], None, None, None, edge[rows, 1:2]]
        for middle, before, after in ((2, 0, 4), (1, 0, 2), (3, 2, 4)):
            ends[middle] = block[rows, middle * HAT : middle * HAT + 1] + 0.5 * (
                ends[before] + ends[after]
            )
        for ky in range(tiles_across):
            values = jnp.where(lane_id == 0, ends[ky], block[rows, ky * HAT : (ky + 1) * HAT])
            result = split_dot(values, hat_y_ref[...], True) + ramp_lanes * ends[ky + 1]
            nodal_ref[2 * ky, rows, :] = result[:, :LANES]
            nodal_ref[2 * ky + 1, rows, :] = result[:, LANES:]
            columns = slice(ky * HAT, (ky + 1) * HAT)
            if part == 0:
                first_rows_ref[:, columns] = result[:HALO]
            if part == height // HAT - 1:
                last_rows_ref[:, columns] = result[-HALO:]
            if ky == 0:
                left_ref[:, rows] = result[:, :LANES].T[:HALO]
            if ky == tiles_across - 1:
                right_ref[:, rows] = result[:, LANES:].T[-HALO:]


def refine_block(source, rank, incoming, share, weight, hat_x, hat_y, height, width, tile_rows, capacity):
    vmem = pl.BlockSpec(memory_space=pltpu.VMEM)
    smem = pl.BlockSpec(memory_space=pltpu.SMEM)
    shapes = [(width // LANES, height, LANES)] + [(HALO, width)] * 2 + [(HALO, height)] * 2
    return pl.pallas_call(
        functools.partial(refine_kernel, width // HAT, tile_rows, capacity),
        out_shape=[jax.ShapeDtypeStruct(shape, jnp.float32) for shape in shapes],
        in_specs=[smem, smem, pl.BlockSpec(memory_space=pltpu.HBM)] + [vmem] * 4,
        out_specs=[vmem] * len(shapes),
        scratch_shapes=[
            pltpu.VMEM((height, width), jnp.float32),
            pltpu.VMEM((height, LANES), jnp.float32),
            pltpu.VMEM((source.shape[0], 2 * tile_rows, LANES), jnp.float32),
            pltpu.VMEM((incoming.shape[0], share.shape[2], LANES), jnp.float32),
            pltpu.SemaphoreType.DMA((4,)),
            pltpu.SemaphoreType.DMA,
        ],
        compiler_params=pltpu.CompilerParams(vmem_limit_bytes=VMEM_LIMIT),
        name="refine_block",
    )(source, rank, incoming, share, weight, hat_x, hat_y)


def fill_halo(target, height, width, above, below, left, right, above_side, below_side):
    tiles = width // LANES
    first = 2 * HALO
    end = first + height
    for t in range(tiles):
        target[t, HALO:first, :] = above[:, t * LANES : (t + 1) * LANES]
        target[t, end : end + HALO, :] = below[:, t * LANES : (t + 1) * LANES]
    between = jnp.zeros((LANES - 2 * HALO, height), jnp.float32)
    target[tiles, first:end, :] = jnp.concatenate([right, between, left], axis=0).T
    target[tiles, HALO:first, :] = above_side
    target[tiles, end : end + HALO, :] = below_side


def edges_kernel(*refs):
    first_rows, last_rows, first_cols, last_cols = refs[8:]
    for f in range(2):
        top, bottom, left, right = refs[4 * f : 4 * f + 4]
        first_rows[f] = top[...]
        last_rows[f] = bottom[...]
        first_cols[f] = left[...].T[:HALO]
        last_cols[f] = right[...].T[-HALO:]


def edges(x, y):
    height, width = x.shape
    specs = [
        pl.BlockSpec((HALO, width), lambda i: (0, 0)),
        pl.BlockSpec((HALO, width), lambda i: (height // HALO - 1, 0)),
        pl.BlockSpec((height, LANES), lambda i: (0, 0)),
        pl.BlockSpec((height, LANES), lambda i: (0, width // LANES - 1)),
    ]
    shapes = [(2, HALO, width)] * 2 + [(2, HALO, height)] * 2
    return pl.pallas_call(
        edges_kernel,
        grid=(1,),
        out_shape=[jax.ShapeDtypeStruct(shape, jnp.float32) for shape in shapes],
        in_specs=specs * 2,
        out_specs=[pl.BlockSpec(shape, lambda i: (0, 0, 0)) for shape in shapes],
        name="velocity_edges",
    )(*[x] * 4, *[y] * 4)


def steps_kernel(
    chunk, last_chunk, nodal_ref, x_ref, y_ref, stencil_ref, rows_above, rows_below, speed_above,
    speed_below, speed_left, speed_right, from_left, from_right, out_ref, field, middle, speed, result_ref, sem,
):
    tiles, height, _ = nodal_ref.shape
    width = tiles * LANES
    count = tiles + 1
    scale = TIME_STEP * DIFFUSION / 12.0
    speed_scale = TIME_STEP / 12.0
    side = lax.broadcasted_iota(jnp.int32, (HALO, LANES), 1)

    def corner(k):
        part = slice(height + k * LANES, height + (k + 1) * LANES)
        return jnp.where(side < LANES // 2, from_right[:, part], from_left[:, part])

    for t in range(tiles):
        field[t, 2 * HALO : 2 * HALO + height, :] = nodal_ref[t]
    fill_halo(
        field, height, width, rows_above, rows_below, from_left[:, :height], from_right[:, :height],
        corner(0), corner(1),
    )
    for f, velocity in enumerate((x_ref, y_ref)):
        for t in range(tiles):
            speed[f, t, 2 * HALO : 2 * HALO + height, :] = (
                velocity[:, t * LANES : (t + 1) * LANES] * speed_scale
            )
        fill_halo(
            speed.at[f], height, width, speed_above[f] * speed_scale, speed_below[f] * speed_scale,
            speed_left[f] * speed_scale, speed_right[f] * speed_scale,
            corner(2 + 2 * f) * speed_scale, corner(3 + 2 * f) * speed_scale,
        )

    def advance(source, start, size, tile_range, store):
        parts = {}
        lane = lax.broadcasted_iota(jnp.int32, (size, LANES), 1)

        def split(t):
            if t not in parts:
                value = source[t, pl.ds(start, size), :]
                high = value.astype(jnp.bfloat16)
                parts[t] = (high, (value - high.astype(jnp.float32)).astype(jnp.bfloat16))
            return parts[t]

        for t in tile_range:
            before, after = split((t - 1) % count), split((t + 1) % count)
            around = [jnp.where(lane >= LANES // 2, b, a) for b, a in zip(before, after)]
            across = jnp.dot(
                jnp.concatenate([*split(t), *around], axis=1),
                stencil_ref[...],
                preferred_element_type=jnp.float32,
            )
            one_below = source[t, pl.ds(start - 1, size), :]
            one_above = source[t, pl.ds(start + 1, size), :]
            two_below = source[t, pl.ds(start - 2, size), :]
            two_above = source[t, pl.ds(start + 2, size), :]
            curve = 16.0 * (one_above + one_below) - (two_above + two_below) + across[:, :LANES]
            slope = 8.0 * (one_above - one_below) - (two_above - two_below)
            result = scale * curve - speed[0, t, pl.ds(start, size), :] * slope
            store(t, result - speed[1, t, pl.ds(start, size), :] * across[:, LANES:])

    def first_half(c, carry):
        start = pl.multiple_of(HALO + c * chunk, HALO)

        def store(t, result):
            middle[t, pl.ds(start, chunk), :] = result

        advance(field, start, chunk, range(count), store)
        return carry

    def second_half(c, carry):
        start = pl.multiple_of(HALO + c * chunk, HALO)

        def store(t, result):
            field[t, pl.ds(start, chunk), :] = 0.5 * (field[t, pl.ds(start, chunk), :] + result)

        advance(middle, start, chunk, range(count), store)
        return carry

    def last_half(c, carry):
        start = pl.multiple_of(2 * HALO + c * last_chunk, HALO)
        place = pl.multiple_of(c * last_chunk, HALO)

        def store(t, result):
            result_ref[pl.ds(place, last_chunk), t * LANES : (t + 1) * LANES] = 0.5 * (
                field[t, pl.ds(start, last_chunk), :] + result
            )

        advance(middle, start, last_chunk, range(tiles), store)
        rows = pl.ds(place, last_chunk)
        pltpu.make_async_copy(result_ref.at[rows], out_ref.at[rows], sem).start()
        return carry

    extended = (height + 2 * HALO) // chunk
    for step in range(STEPS):
        lax.fori_loop(0, extended, first_half, 0)
        if step < STEPS - 1:
            lax.fori_loop(0, extended, second_half, 0)
    lax.fori_loop(0, height // last_chunk, last_half, 0)
    pltpu.make_async_copy(result_ref, out_ref, sem).wait()


def largest_chunk(rows, limit):
    return max(size for size in range(16, limit + 1, 16) if rows % size == 0)


def run_steps(nodal, x, y, stencil, *halo):
    tiles, height, _ = nodal.shape
    vmem = pl.BlockSpec(memory_space=pltpu.VMEM)
    extended = (tiles + 1, height + 4 * HALO, LANES)
    return pl.pallas_call(
        functools.partial(
            steps_kernel, largest_chunk(height + 2 * HALO, 192), largest_chunk(height, 192)
        ),
        out_shape=jax.ShapeDtypeStruct((height, tiles * LANES), jnp.float32),
        in_specs=[vmem] * (4 + len(halo)),
        out_specs=pl.BlockSpec(memory_space=pl.ANY),
        scratch_shapes=[
            pltpu.VMEM(extended, jnp.float32),
            pltpu.VMEM(extended, jnp.float32),
            pltpu.VMEM((2,) + extended, jnp.float32),
            pltpu.VMEM((height, tiles * LANES), jnp.float32),
            pltpu.SemaphoreType.DMA,
        ],
        compiler_params=pltpu.CompilerParams(vmem_limit_bytes=VMEM_LIMIT),
        name="heun_steps",
    )(nodal, x, y, stencil, *halo)


def stencil_matrix():
    row = lax.broadcasted_iota(jnp.int32, (4 * LANES, 2 * LANES), 0)
    column = lax.broadcasted_iota(jnp.int32, (4 * LANES, 2 * LANES), 1)
    lane = row % LANES
    outside = jnp.where(lane < LANES // 2, lane + LANES, lane - LANES)
    shift = jnp.where(row < 2 * LANES, lane, outside) - column % LANES
    distance = jnp.abs(shift)
    centre = 12.0 / (TIME_STEP * DIFFUSION) - 60.0
    curve = jnp.where(distance == 1, 16.0, jnp.where(distance == 2, -1.0, 0.0))
    curve = jnp.where(distance == 0, centre, curve)
    slope = jnp.where(distance == 1, 8.0, jnp.where(distance == 2, -1.0, 0.0)) * jnp.sign(
        shift
    ).astype(jnp.float32)
    return jnp.where(column < LANES, curve, slope).astype(jnp.bfloat16)


def hat_matrix(size):
    place = lax.broadcasted_iota(jnp.int32, (size, size), 0)
    node = lax.broadcasted_iota(jnp.int32, (size, size), 1)
    return jnp.where(node == 0, 1.0 - place.astype(jnp.float32) / size, hat_value(node, place))


def hat_value(node, place):
    spacing = jnp.maximum(node & (-node), 1).astype(jnp.float32)
    return jnp.maximum(0.0, 1.0 - jnp.abs(place - node).astype(jnp.float32) / spacing)


def coarse_share(node, place):
    return jnp.where(node == 0, 1.0, hat_value(node, place))


def weight_pattern(grid_levels, coefficients, faulty_grids):
    grid_ids = jnp.arange(coefficients.shape[0], dtype=jnp.int32)
    alive = jnp.all(faulty_grids[None, :] != grid_ids[:, None], axis=1)
    share = jnp.where(alive, coefficients, 0).astype(jnp.float32)
    row = lax.broadcasted_iota(jnp.int32, (8, LANES), 0)[None]
    lane = lax.broadcasted_iota(jnp.int32, (8, LANES), 1)[None]
    mask_x = (jnp.int32(1) << grid_levels[:, 0]) - 1
    mask_y = (jnp.int32(1) << grid_levels[:, 1]) - 1
    covered = ((row & mask_x[:, None, None]) == 0) & ((lane & mask_y[:, None, None]) == 0)
    return jnp.sum(jnp.where(covered, share[:, None, None], 0.0), axis=0)


def shifted(array, axis, by):
    size = lax.axis_size(axis)
    return lax.ppermute(array, axis, [(i, (i + by) % size) for i in range(size)])


def lead_share(offsets, index_x, index_y, size_x, size_y, tiles_across, tile_height):
    devices = size_x * size_y
    row_parts = 2 * tiles_across
    by_row = jnp.repeat(offsets[:tiles_across], 2)[:, None]
    by_col = jnp.repeat(offsets[::tiles_across], tile_height).reshape(-1, LANES)
    spread_row = jnp.broadcast_to(by_row, (row_parts, LANES))
    spread_corner = jnp.broadcast_to(offsets[0], (4, LANES))
    table = jnp.concatenate([spread_row, by_col, spread_corner], axis=0)
    owner = lax.broadcasted_iota(jnp.int32, (devices, 1, 1), 0)
    block = (owner - table[None]) % devices
    x, y = block // size_y, block % size_y
    line = lax.broadcasted_iota(jnp.int32, (1, table.shape[0], 1), 1)
    corner = line - (table.shape[0] - 4)
    shares = []
    for by in range(2):
        rows = jnp.where(y == index_y, coarse_share(x, index_x + by), 0.0)
        cols = jnp.where(x == index_x, coarse_share(y, index_y + by), 0.0)
        corners = coarse_share(x, index_x + corner // 2) * coarse_share(y, index_y + corner % 2)
        shares.append(
            jnp.where(line < row_parts, rows, jnp.where(corner < 0, cols, corners))
        )
    return jnp.stack(shares)


def local(
    owned_surplus, tile_owner, grid_levels, coefficients, faulty_grids, velocity_x, velocity_y
):
    slot_count, tile_height, tile_width = owned_surplus.shape
    rows_local, cols_local = velocity_x.shape
    size_x = lax.axis_size("gx")
    size_y = lax.axis_size("gy")
    device_count = size_x * size_y
    capacity = 2 * slot_count // device_count
    tiles_across = cols_local // tile_width
    index_x = lax.axis_index("gx")
    index_y = lax.axis_index("gy")
    own_index = index_x * size_y + index_y
    offsets = tile_owner[:slot_count]
    positions = jnp.arange(slot_count, dtype=jnp.int32)
    same_offset = offsets[:, None] == offsets[None, :]
    earlier = positions[None, :] < positions[:, None]
    slot_rank = jnp.sum((same_offset & earlier).astype(jnp.int32), axis=1)
    source = (own_index + offsets) % device_count
    outgoing = pack(tile_owner, owned_surplus, device_count, capacity, tiles_across)
    incoming = lax.all_to_all(outgoing, ("gx", "gy"), split_axis=0, concat_axis=0, tiled=True)

    first_rows, last_rows, first_cols, last_cols = edges(velocity_x, velocity_y)
    speed_halo = (
        shifted(last_rows, "gx", 1),
        shifted(first_rows, "gx", -1),
        shifted(last_cols, "gy", 1),
        shifted(first_cols, "gy", -1),
    )
    incoming, speed_halo = lax.optimization_barrier((incoming, speed_halo))
    share = lead_share(offsets, index_x, index_y, size_x, size_y, tiles_across, tile_height)
    weight = weight_pattern(grid_levels, coefficients, faulty_grids)
    hat = hat_matrix(HAT).astype(jnp.bfloat16)

    nodal, first_rows, last_rows, first_cols, last_cols = refine_block(
        source, slot_rank, incoming, share, weight, hat, hat.T, rows_local, cols_local, tile_height,
        capacity,
    )
    above = shifted(last_rows, "gx", 1)
    below = shifted(first_rows, "gx", -1)
    strips = [above, below] + [side[f] for f in range(2) for side in speed_halo[:2]]
    from_left = shifted(
        jnp.concatenate([last_cols] + [strip[:, -LANES:] for strip in strips], axis=1), "gy", 1
    )
    from_right = shifted(
        jnp.concatenate([first_cols] + [strip[:, :LANES] for strip in strips], axis=1), "gy", -1
    )
    return run_steps(
        nodal, velocity_x, velocity_y, stencil_matrix(), above, below, *speed_halo, from_left, from_right
    )


def solution(mesh):
    return jax.shard_map(
        local,
        mesh=mesh,
        in_specs=(P(("gx", "gy"), None, None), P(), P(), P(), P(), P("gx", "gy"), P("gx", "gy")),
        out_specs=P("gx", "gy"),
        check_vma=False,
    )
```

```python
import functools

import jax
import jax.numpy as jnp
from jax import lax
from jax.experimental import pallas as pl
from jax.experimental.pallas import tpu as pltpu
from jax.sharding import PartitionSpec as P

STEPS = 2
TIME_STEP = 0.2
DIFFUSION = 0.5
HALO = 8
LANES = 128
HAT = 256
VMEM_LIMIT = 24 << 20
PACK_LIMIT = 60 << 20


def pack_kernel(
    tiles_across, capacity, owner_ref, owned_ref, outgoing_ref, staged, wide, leads, offsets, used,
    sem_in, sem_out, sem_lead, sem_owner,
):
    count, tile_rows, _ = owned_ref.shape
    messages = outgoing_ref.shape[0]
    size = 2 * tile_rows
    groups = sem_in.shape[0]
    per_group = count // groups

    def arrival(g):
        part = pl.ds(g * per_group, per_group)
        return pltpu.make_async_copy(owned_ref.at[part], staged.at[part], sem_in.at[g])

    head = pltpu.make_async_copy(owner_ref.at[pl.ds(0, count)], offsets, sem_owner)
    head.start()
    for g in range(groups):
        arrival(g).start()
    own_index = lax.axis_index("gx") * lax.axis_size("gy") + lax.axis_index("gy")

    def clear(m, carry):
        used[m] = 0
        return carry

    lax.fori_loop(0, messages, clear, 0, unroll=8)
    head.wait()
    for g in range(groups):
        arrival(g).wait()

        def place(i, carry, g=g):
            k = g * per_group + i
            wide[k, :tile_rows, :] = staged[k, :, :LANES]
            wide[k, tile_rows:, :] = staged[k, :, LANES:]
            offset = offsets[k]
            rank = used[offset]
            used[offset] = rank + 1
            target = lax.rem(own_index - offset + messages, messages)
            row = pl.multiple_of(rank * size, size)
            pltpu.make_async_copy(
                wide.at[k], outgoing_ref.at[target, pl.ds(row, size), :], sem_out
            ).start()
            return carry

        lax.fori_loop(0, per_group, place, 0, unroll=8)

    rows = []
    for ky in range(tiles_across):
        rows += [staged[ky, 0:1, :LANES], staged[ky, 0:1, LANES:]]
    per_part = LANES // tile_rows
    for part in range(count // tiles_across // per_part):
        columns = [staged[(part * per_part + t) * tiles_across, :, :LANES] for t in range(per_part)]
        rows.append(jnp.concatenate(columns, axis=0).T[0:1])
    rows += [rows[0]] * 4
    lead = jnp.concatenate(rows, axis=0)

    def address(m, carry):
        leads[m] = lead
        return carry

    lax.fori_loop(0, messages, address, 0, unroll=8)
    to_all = pltpu.make_async_copy(
        leads, outgoing_ref.at[:, pl.ds(size * capacity, lead.shape[0]), :], sem_lead
    )
    to_all.start()
    to_all.wait()
    pltpu.make_async_copy(wide, wide, sem_out).wait()


def pack(tile_owner, owned, messages, capacity, tiles_across):
    count, tile_rows, _ = owned.shape
    lead_rows = 2 * tiles_across + count // tiles_across * tile_rows // LANES + 4
    anywhere = pl.BlockSpec(memory_space=pl.ANY)
    return pl.pallas_call(
        functools.partial(pack_kernel, tiles_across, capacity),
        out_shape=jax.ShapeDtypeStruct(
            (messages, capacity * tile_rows * 2 + lead_rows, LANES), owned.dtype
        ),
        in_specs=[anywhere, anywhere],
        out_specs=anywhere,
        scratch_shapes=[
            pltpu.VMEM(owned.shape, owned.dtype),
            pltpu.VMEM((count, 2 * tile_rows, LANES), owned.dtype),
            pltpu.VMEM((messages, lead_rows, LANES), owned.dtype),
            pltpu.SMEM((count,), jnp.int32),
            pltpu.SMEM((messages,), jnp.int32),
            pltpu.SemaphoreType.DMA((8,)),
            pltpu.SemaphoreType.DMA,
            pltpu.SemaphoreType.DMA,
            pltpu.SemaphoreType.DMA,
        ],
        compiler_params=pltpu.CompilerParams(vmem_limit_bytes=PACK_LIMIT),
        name="pack_tiles",
    )(tile_owner, owned)


def split_dot(left, right, split_left):
    value = left if split_left else right
    high = value.astype(jnp.bfloat16)
    low = (value - high.astype(jnp.float32)).astype(jnp.bfloat16)
    if split_left:
        pairs = ((high, right), (low, right))
    else:
        pairs = ((left, high), (left, low))
    return sum(jnp.dot(a, b, preferred_element_type=jnp.float32) for a, b in pairs)


def refine_kernel(
    tiles_across, tile_rows, capacity, source_ref, rank_ref, incoming_ref, share_ref, weight_ref,
    hat_x_ref, hat_y_ref, nodal_ref, first_rows_ref, last_rows_ref, left_ref, right_ref,
    block, edge, staged, leads, sem_tile, sem_lead,
):
    height = nodal_ref.shape[1]
    tiles_down = height // tile_rows
    row_parts = 2 * tiles_across
    col_parts = height // LANES
    lead_row = 2 * tile_rows * capacity
    lead_size = share_ref.shape[2]
    tile_weight = jnp.concatenate([weight_ref[...]] * (tile_rows // 8), axis=0)
    size = 2 * tile_rows
    groups = sem_tile.shape[0]
    per_group = tiles_down * tiles_across // groups
    lead_copy = pltpu.make_async_copy(
        incoming_ref.at[:, pl.ds(lead_row, lead_size), :], leads, sem_lead
    )
    lead_copy.start()
    for g in range(groups):

        def fetch(i, carry, g=g):
            k = g * per_group + i
            row = pl.multiple_of(rank_ref[k] * size, size)
            pltpu.make_async_copy(
                incoming_ref.at[source_ref[k], pl.ds(row, size), :], staged.at[k], sem_tile.at[g]
            ).start()
            return carry

        lax.fori_loop(0, per_group, fetch, 0, unroll=8)
    lead_copy.wait()

    def collect(m, sums):
        lead = leads[m]
        return tuple(total + share_ref[i, m] * lead for i, total in enumerate(sums))

    zero = jnp.zeros((lead_size, LANES), jnp.float32)
    own_lead, next_lead = lax.fori_loop(0, leads.shape[0], collect, (zero, zero), unroll=8)

    weight = weight_ref[...]
    lane = lax.broadcasted_iota(jnp.int32, (1, LANES), 1)
    corner_base = row_parts + col_parts
    corner = lambda x: weight[0:1, 0:1] * jnp.where(
        lane == 0,
        own_lead[corner_base + 2 * x : corner_base + 2 * x + 1, 0:1],
        own_lead[corner_base + 2 * x + 1 : corner_base + 2 * x + 2, 0:1],
    )
    for part in range(col_parts):
        pair = jnp.concatenate(
            [
                own_lead[row_parts + part : row_parts + part + 1],
                next_lead[row_parts + part : row_parts + part + 1],
                jnp.zeros((LANES - 2, LANES), jnp.float32),
            ],
            axis=0,
        ).T
        edge[part * LANES : (part + 1) * LANES, :] = (
            pair.reshape(LANES // 8, 8, LANES) * weight[:, 0:1][None]
        ).reshape(LANES, LANES)

    row_id = lax.broadcasted_iota(jnp.int32, (HAT, HAT), 0)
    lane_id = lax.broadcasted_iota(jnp.int32, (HAT, HAT), 1)
    ramp_rows = row_id.astype(jnp.float32) * (1.0 / HAT)
    ramp_lanes = lane_id.astype(jnp.float32) * (1.0 / HAT)

    def refine_down(target, lanes, own, after):
        width = own.shape[1]
        middle = target[HAT : HAT + 1, lanes] + 0.5 * (own + after)
        for part, (first, last) in enumerate(((own, middle), (middle, after))):
            rows = slice(part * HAT, (part + 1) * HAT)
            values = jnp.where(row_id[:, :width] == 0, first, target[rows, lanes])
            target[rows, lanes] = split_dot(hat_x_ref[...], values, False) + ramp_rows[:, :width] * last

    refine_down(edge, slice(0, LANES), corner(0), corner(1))

    def place(kx, carry):
        row = pl.multiple_of(kx * tile_rows, tile_rows)
        for ky in range(tiles_across):
            for part in range(2):
                block[pl.ds(row, tile_rows), (2 * ky + part) * LANES : (2 * ky + part + 1) * LANES] = (
                    staged[kx * tiles_across + ky, part * tile_rows : (part + 1) * tile_rows, :]
                    * tile_weight
                )
        return carry

    for g in range(groups):
        part = staged.at[pl.ds(g * per_group, per_group)]
        pltpu.make_async_copy(part, part, sem_tile.at[g]).wait()
        lax.fori_loop(
            g * tiles_down // groups, (g + 1) * tiles_down // groups, place, 0, unroll=2
        )
    line = lambda lead, ky: (
        jnp.concatenate([lead[2 * ky : 2 * ky + 1], lead[2 * ky + 1 : 2 * ky + 2]], axis=1)
        * jnp.concatenate([weight[0:1]] * 2, axis=1)
    )
    for ky in range(tiles_across):
        refine_down(
            block, slice(ky * HAT, (ky + 1) * HAT), line(own_lead, ky), line(next_lead, ky)
        )
    for part in range(height // HAT):
        rows = slice(part * HAT, (part + 1) * HAT)
        ends = [edge[rows, 0:1], None, None, None, edge[rows, 1:2]]
        for middle, before, after in ((2, 0, 4), (1, 0, 2), (3, 2, 4)):
            ends[middle] = block[rows, middle * HAT : middle * HAT + 1] + 0.5 * (
                ends[before] + ends[after]
            )
        for ky in range(tiles_across):
            values = jnp.where(lane_id == 0, ends[ky], block[rows, ky * HAT : (ky + 1) * HAT])
            result = split_dot(values, hat_y_ref[...], True) + ramp_lanes * ends[ky + 1]
            nodal_ref[2 * ky, rows, :] = result[:, :LANES]
            nodal_ref[2 * ky + 1, rows, :] = result[:, LANES:]
            columns = slice(ky * HAT, (ky + 1) * HAT)
            if part == 0:
                first_rows_ref[:, columns] = result[:HALO]
            if part == height // HAT - 1:
                last_rows_ref[:, columns] = result[-HALO:]
            if ky == 0:
                left_ref[:, rows] = result[:, :LANES].T[:HALO]
            if ky == tiles_across - 1:
                right_ref[:, rows] = result[:, LANES:].T[-HALO:]


def refine_block(source, rank, incoming, share, weight, hat_x, hat_y, height, width, tile_rows, capacity):
    vmem = pl.BlockSpec(memory_space=pltpu.VMEM)
    smem = pl.BlockSpec(memory_space=pltpu.SMEM)
    shapes = [(width // LANES, height, LANES)] + [(HALO, width)] * 2 + [(HALO, height)] * 2
    return pl.pallas_call(
        functools.partial(refine_kernel, width // HAT, tile_rows, capacity),
        out_shape=[jax.ShapeDtypeStruct(shape, jnp.float32) for shape in shapes],
        in_specs=[smem, smem, pl.BlockSpec(memory_space=pltpu.HBM)] + [vmem] * 4,
        out_specs=[vmem] * len(shapes),
        scratch_shapes=[
            pltpu.VMEM((height, width), jnp.float32),
            pltpu.VMEM((height, LANES), jnp.float32),
            pltpu.VMEM((source.shape[0], 2 * tile_rows, LANES), jnp.float32),
            pltpu.VMEM((incoming.shape[0], share.shape[2], LANES), jnp.float32),
            pltpu.SemaphoreType.DMA((4,)),
            pltpu.SemaphoreType.DMA,
        ],
        compiler_params=pltpu.CompilerParams(vmem_limit_bytes=VMEM_LIMIT),
        name="refine_block",
    )(source, rank, incoming, share, weight, hat_x, hat_y)


def split(value):
    high = value.astype(jnp.bfloat16)
    return high, (value - high.astype(jnp.float32)).astype(jnp.bfloat16)


def heun_loops(
    field, middle, speed, height, chunk, last_chunk, make_across, store_last, after_last
):
    count = field.shape[0]
    scale = TIME_STEP * DIFFUSION / 12.0

    def advance(source, start, size, store):
        across_of = make_across(source, start, size)
        for t in range(count):
            across = across_of(t)
            one_below = source[t, pl.ds(start - 1, size), :]
            one_above = source[t, pl.ds(start + 1, size), :]
            two_below = source[t, pl.ds(start - 2, size), :]
            two_above = source[t, pl.ds(start + 2, size), :]
            curve = 16.0 * (one_above + one_below) - (two_above + two_below) + across[:, :LANES]
            slope = 8.0 * (one_above - one_below) - (two_above - two_below)
            result = scale * curve - speed[0, t, pl.ds(start, size), :] * slope
            store(t, result - speed[1, t, pl.ds(start, size), :] * across[:, LANES:])

    def first_half(c, carry):
        start = pl.multiple_of(HALO + c * chunk, HALO)

        def store(t, result):
            middle[t, pl.ds(start, chunk), :] = result

        advance(field, start, chunk, store)
        return carry

    def second_half(c, carry):
        start = pl.multiple_of(HALO + c * chunk, HALO)

        def store(t, result):
            field[t, pl.ds(start, chunk), :] = 0.5 * (field[t, pl.ds(start, chunk), :] + result)

        advance(middle, start, chunk, store)
        return carry

    def last_half(c, carry):
        start = pl.multiple_of(2 * HALO + c * last_chunk, HALO)
        place = pl.ds(pl.multiple_of(c * last_chunk, HALO), last_chunk)

        def store(t, result):
            store_last(t, place, 0.5 * (field[t, pl.ds(start, last_chunk), :] + result))

        advance(middle, start, last_chunk, store)
        after_last(place)
        return carry

    extended = (height + 2 * HALO) // chunk
    for step in range(STEPS):
        lax.fori_loop(0, extended, first_half, 0)
        if step < STEPS - 1:
            lax.fori_loop(0, extended, second_half, 0)
    lax.fori_loop(0, height // last_chunk, last_half, 0)


def largest_chunk(rows, limit):
    return max(size for size in range(16, limit + 1, 16) if rows % size == 0)


def chunks(height):
    return largest_chunk(height + 2 * HALO, 192), largest_chunk(height, 192)


def main_kernel(
    nodal_ref, speed, stencil_ref, rows_above, rows_below, out_ref, field, middle, result_ref, sem
):
    tiles, height, _ = nodal_ref.shape
    first, end = 2 * HALO, 2 * HALO + height
    for t in range(tiles):
        lanes = slice(t * LANES, (t + 1) * LANES)
        field[t, first:end, :] = nodal_ref[t]
        field[t, HALO:first, :] = rows_above[:, lanes]
        field[t, end : end + HALO, :] = rows_below[:, lanes]

    def make_across(source, start, size):
        parts = {}
        lane = lax.broadcasted_iota(jnp.int32, (size, LANES), 1)

        def part(t):
            if t not in parts:
                parts[t] = split(source[t, pl.ds(start, size), :])
            return parts[t]

        def across_of(t):
            before, after = part((t - 1) % tiles), part((t + 1) % tiles)
            around = [jnp.where(lane >= LANES // 2, b, a) for b, a in zip(before, after)]
            return jnp.dot(
                jnp.concatenate([*part(t), *around], axis=1),
                stencil_ref[...],
                preferred_element_type=jnp.float32,
            )

        return across_of

    def store_last(t, place, value):
        result_ref[place, t * LANES : (t + 1) * LANES] = value

    def after_last(place):
        pltpu.make_async_copy(result_ref.at[place], out_ref.at[place], sem).start()

    heun_loops(
        field, middle, speed, height, *chunks(height), make_across, store_last, after_last
    )
    pltpu.make_async_copy(result_ref, out_ref, sem).wait()


def main_steps(nodal, speed, stencil, above, below):
    tiles, height, _ = nodal.shape
    vmem = pl.BlockSpec(memory_space=pltpu.VMEM)
    extended = (tiles, height + 4 * HALO, LANES)
    cells = height * tiles * LANES
    return pl.pallas_call(
        main_kernel,
        out_shape=jax.ShapeDtypeStruct((height, tiles * LANES), jnp.float32),
        in_specs=[vmem] * 5,
        out_specs=pl.BlockSpec(memory_space=pl.ANY),
        scratch_shapes=[
            pltpu.VMEM(extended, jnp.float32),
            pltpu.VMEM(extended, jnp.float32),
            pltpu.VMEM((height, tiles * LANES), jnp.float32),
            pltpu.SemaphoreType.DMA,
        ],
        compiler_params=pltpu.CompilerParams(vmem_limit_bytes=VMEM_LIMIT),
        cost_estimate=pl.CostEstimate(
            flops=4 * 2 * cells * 8 * LANES, bytes_accessed=16 * cells, transcendentals=0
        ),
        name="heun_main",
    )(nodal, speed, stencil, above, below)


def mix(i, inner, outer):
    lower = lax.broadcasted_iota(jnp.int32, inner.shape, inner.ndim - 1) < LANES // 2
    return jnp.where(lower, inner, outer) if i == 0 else jnp.where(lower, outer, inner)


def outer_columns(i, columns):
    rest = jnp.zeros((LANES - HALO, columns.shape[1]), jnp.float32)
    return jnp.concatenate([rest, columns] if i == 0 else [columns, rest], axis=0).T


def spread_kernel(
    x_ref, y_ref, above_ref, below_ref, left_ref, right_ref, speed_ref, rim_ref
):
    height, width = x_ref.shape
    first, end = 2 * HALO, 2 * HALO + height
    scale = TIME_STEP / 12.0
    for f, velocity in enumerate((x_ref, y_ref)):
        for t in range(width // LANES):
            lanes = slice(t * LANES, (t + 1) * LANES)
            speed_ref[f, t, first:end, :] = velocity[:, lanes] * scale
            speed_ref[f, t, HALO:first, :] = above_ref[f, :, lanes] * scale
            speed_ref[f, t, end : end + HALO, :] = below_ref[f, :, lanes] * scale
        for i, received in enumerate((left_ref, right_ref)):
            lanes = slice(i * (width - LANES), i * (width - LANES) + LANES)
            outer = outer_columns(i, received[f])
            rim_ref[f, i, first:end, :] = mix(i, velocity[:, lanes], outer) * scale
            rim_ref[f, i, HALO:first, :] = above_ref[f, :, lanes] * scale
            rim_ref[f, i, end : end + HALO, :] = below_ref[f, :, lanes] * scale


def spread(x, y, *halo):
    height, width = x.shape
    vmem = pl.BlockSpec(memory_space=pltpu.VMEM)
    rows = height + 4 * HALO
    return pl.pallas_call(
        spread_kernel,
        out_shape=[
            jax.ShapeDtypeStruct((2, width // LANES, rows, LANES), jnp.float32),
            jax.ShapeDtypeStruct((2, 2, rows, LANES), jnp.float32),
        ],
        in_specs=[vmem] * (2 + len(halo)),
        out_specs=[vmem, vmem],
        compiler_params=pltpu.CompilerParams(vmem_limit_bytes=VMEM_LIMIT),
        cost_estimate=pl.CostEstimate(
            flops=4 * height * width, bytes_accessed=20 * height * width, transcendentals=0
        ),
        name="spread_velocity",
    )(x, y, *halo)


def rim_kernel(
    main_ref, nodal_ref, rim_ref, stencil_ref, rows_above, rows_below, from_left, from_right, out_ref,
    field, middle, speed, result_ref, sem,
):
    tiles, height, _ = nodal_ref.shape
    width = tiles * LANES
    first, end = 2 * HALO, 2 * HALO + height
    sides = (slice(0, LANES), slice(width - LANES, width))
    fetches = [
        pltpu.make_async_copy(main_ref.at[:, pl.ds(side.start, LANES)], result_ref.at[i], sem.at[i])
        for i, side in enumerate(sides)
    ]
    for fetch in fetches:
        fetch.start()

    def corner(received, k):
        return received[:, height + k * LANES : height + (k + 1) * LANES]

    for i, (side, received) in enumerate(zip(sides, (from_left, from_right))):
        field[i, first:end, :] = mix(
            i, nodal_ref[i * (tiles - 1)], outer_columns(i, received[:, :height])
        )
        field[i, HALO:first, :] = mix(i, rows_above[:, side], corner(received, 0))
        field[i, end : end + HALO, :] = mix(i, rows_below[:, side], corner(received, 1))
        for f in range(2):
            speed[f, i, first:end, :] = rim_ref[f, i, first:end, :]
            for k, rows in enumerate((slice(HALO, first), slice(end, end + HALO))):
                speed[f, i, rows, :] = mix(
                    i, rim_ref[f, i, rows, :], corner(received, 2 + 2 * f + k) * (TIME_STEP / 12.0)
                )
    for fetch in fetches:
        fetch.wait()

    def make_across(source, start, size):
        def across_of(t):
            return jnp.dot(
                jnp.concatenate(split(source[t, pl.ds(start, size), :]), axis=1),
                stencil_ref[...],
                preferred_element_type=jnp.float32,
            )

        return across_of

    def store_last(t, place, value):
        lane = lax.broadcasted_iota(jnp.int32, value.shape, 1)
        wanted = lane < HALO if t == 0 else lane >= LANES - HALO
        result_ref[t, place, :] = jnp.where(wanted, value, result_ref[t, place, :])

    heun_loops(
        field, middle, speed, height, *chunks(height), make_across, store_last, lambda place: None
    )
    stores = [
        pltpu.make_async_copy(result_ref.at[i], out_ref.at[:, pl.ds(side.start, LANES)], sem.at[i])
        for i, side in enumerate(sides)
    ]
    for store in stores:
        store.start()
    for store in stores:
        store.wait()


def rim_steps(main, nodal, speed, stencil, *halo):
    _, height, _ = nodal.shape
    vmem = pl.BlockSpec(memory_space=pltpu.VMEM)
    anywhere = pl.BlockSpec(memory_space=pl.ANY)
    extended = (2, height + 4 * HALO, LANES)
    return pl.pallas_call(
        rim_kernel,
        out_shape=jax.ShapeDtypeStruct(main.shape, jnp.float32),
        in_specs=[anywhere] + [vmem] * (3 + len(halo)),
        out_specs=anywhere,
        input_output_aliases={0: 0},
        scratch_shapes=[
            pltpu.VMEM(extended, jnp.float32),
            pltpu.VMEM(extended, jnp.float32),
            pltpu.VMEM((2,) + extended, jnp.float32),
            pltpu.VMEM((2, height, LANES), jnp.float32),
            pltpu.SemaphoreType.DMA((2,)),
        ],
        compiler_params=pltpu.CompilerParams(vmem_limit_bytes=VMEM_LIMIT),
        name="heun_rim",
    )(main, nodal, speed, stencil, *halo)


def edges_kernel(*refs):
    first_rows, last_rows, first_cols, last_cols = refs[8:]
    for f in range(2):
        top, bottom, left, right = refs[4 * f : 4 * f + 4]
        first_rows[f] = top[...]
        last_rows[f] = bottom[...]
        first_cols[f] = left[...].T[:HALO]
        last_cols[f] = right[...].T[-HALO:]


def edges(x, y):
    height, width = x.shape
    specs = [
        pl.BlockSpec((HALO, width), lambda i: (0, 0)),
        pl.BlockSpec((HALO, width), lambda i: (height // HALO - 1, 0)),
        pl.BlockSpec((height, LANES), lambda i: (0, 0)),
        pl.BlockSpec((height, LANES), lambda i: (0, width // LANES - 1)),
    ]
    shapes = [(2, HALO, width)] * 2 + [(2, HALO, height)] * 2
    return pl.pallas_call(
        edges_kernel,
        grid=(1,),
        out_shape=[jax.ShapeDtypeStruct(shape, jnp.float32) for shape in shapes],
        in_specs=specs * 2,
        out_specs=[pl.BlockSpec(shape, lambda i: (0, 0, 0)) for shape in shapes],
        name="velocity_edges",
    )(*[x] * 4, *[y] * 4)


def stencil_entries(shift, column):
    distance = jnp.abs(shift)
    centre = 12.0 / (TIME_STEP * DIFFUSION) - 60.0
    curve = jnp.where(distance == 1, 16.0, jnp.where(distance == 2, -1.0, 0.0))
    curve = jnp.where(distance == 0, centre, curve)
    slope = jnp.where(distance == 1, 8.0, jnp.where(distance == 2, -1.0, 0.0)) * jnp.sign(
        shift
    ).astype(jnp.float32)
    return jnp.where(column < LANES, curve, slope).astype(jnp.bfloat16)


def stencil_matrices():
    row = lax.broadcasted_iota(jnp.int32, (4 * LANES, 2 * LANES), 0)
    column = lax.broadcasted_iota(jnp.int32, (4 * LANES, 2 * LANES), 1)
    lane = row % LANES
    outside = jnp.where(lane < LANES // 2, lane + LANES, lane - LANES)
    shift = jnp.where(row < 2 * LANES, lane, outside) - column % LANES
    ring = lane - column % LANES
    ring = jnp.where(ring > LANES // 2, ring - LANES, jnp.where(ring < -LANES // 2, ring + LANES, ring))
    return stencil_entries(shift, column), stencil_entries(ring, column)[: 2 * LANES]


def hat_matrix(size):
    place = lax.broadcasted_iota(jnp.int32, (size, size), 0)
    node = lax.broadcasted_iota(jnp.int32, (size, size), 1)
    return jnp.where(node == 0, 1.0 - place.astype(jnp.float32) / size, hat_value(node, place))


def hat_value(node, place):
    spacing = jnp.maximum(node & (-node), 1).astype(jnp.float32)
    return jnp.maximum(0.0, 1.0 - jnp.abs(place - node).astype(jnp.float32) / spacing)


def coarse_share(node, place):
    return jnp.where(node == 0, 1.0, hat_value(node, place))


def weight_pattern(grid_levels, coefficients, faulty_grids):
    grid_ids = jnp.arange(coefficients.shape[0], dtype=jnp.int32)
    alive = jnp.all(faulty_grids[None, :] != grid_ids[:, None], axis=1)
    share = jnp.where(alive, coefficients, 0).astype(jnp.float32)
    row = lax.broadcasted_iota(jnp.int32, (8, LANES), 0)[None]
    lane = lax.broadcasted_iota(jnp.int32, (8, LANES), 1)[None]
    mask_x = (jnp.int32(1) << grid_levels[:, 0]) - 1
    mask_y = (jnp.int32(1) << grid_levels[:, 1]) - 1
    covered = ((row & mask_x[:, None, None]) == 0) & ((lane & mask_y[:, None, None]) == 0)
    return jnp.sum(jnp.where(covered, share[:, None, None], 0.0), axis=0)


def exchange(first, last, axis):
    size = lax.axis_size(axis)
    even = lax.axis_index(axis) % 2 == 0
    inner = [(i, i ^ 1) for i in range(size)]
    outer = [((i + 1) % size, ((i ^ 1) + 1) % size) for i in range(size)]
    by_inner = lax.ppermute(jnp.where(even, last, first), axis, inner)
    by_outer = lax.ppermute(jnp.where(even, first, last), axis, outer)
    return jnp.where(even, by_outer, by_inner), jnp.where(even, by_inner, by_outer)


def lead_share(offsets, index_x, index_y, size_x, size_y, tiles_across, tile_height):
    devices = size_x * size_y
    row_parts = 2 * tiles_across
    by_row = jnp.repeat(offsets[:tiles_across], 2)[:, None]
    by_col = jnp.repeat(offsets[::tiles_across], tile_height).reshape(-1, LANES)
    spread_row = jnp.broadcast_to(by_row, (row_parts, LANES))
    spread_corner = jnp.broadcast_to(offsets[0], (4, LANES))
    table = jnp.concatenate([spread_row, by_col, spread_corner], axis=0)
    owner = lax.broadcasted_iota(jnp.int32, (devices, 1, 1), 0)
    block = (owner - table[None]) % devices
    x, y = block // size_y, block % size_y
    line = lax.broadcasted_iota(jnp.int32, (1, table.shape[0], 1), 1)
    corner = line - (table.shape[0] - 4)
    shares = []
    for by in range(2):
        rows = jnp.where(y == index_y, coarse_share(x, index_x + by), 0.0)
        cols = jnp.where(x == index_x, coarse_share(y, index_y + by), 0.0)
        corners = coarse_share(x, index_x + corner // 2) * coarse_share(y, index_y + corner % 2)
        shares.append(
            jnp.where(line < row_parts, rows, jnp.where(corner < 0, cols, corners))
        )
    return jnp.stack(shares)


def local(
    owned_surplus, tile_owner, grid_levels, coefficients, faulty_grids, velocity_x, velocity_y
):
    slot_count, tile_height, tile_width = owned_surplus.shape
    rows_local, cols_local = velocity_x.shape
    size_x = lax.axis_size("gx")
    size_y = lax.axis_size("gy")
    device_count = size_x * size_y
    capacity = 2 * slot_count // device_count
    tiles_across = cols_local // tile_width
    index_x = lax.axis_index("gx")
    index_y = lax.axis_index("gy")
    own_index = index_x * size_y + index_y
    offsets = tile_owner[:slot_count]
    positions = jnp.arange(slot_count, dtype=jnp.int32)
    same_offset = offsets[:, None] == offsets[None, :]
    earlier = positions[None, :] < positions[:, None]
    slot_rank = jnp.sum((same_offset & earlier).astype(jnp.int32), axis=1)
    source = (own_index + offsets) % device_count
    outgoing = pack(tile_owner, owned_surplus, device_count, capacity, tiles_across)
    incoming = lax.all_to_all(outgoing, ("gx", "gy"), split_axis=0, concat_axis=0, tiled=True)

    first_rows, last_rows, first_cols, last_cols = edges(velocity_x, velocity_y)
    speed_halo = (
        *exchange(first_rows, last_rows, "gx"),
        *exchange(first_cols, last_cols, "gy"),
    )
    incoming, speed_halo = lax.optimization_barrier((incoming, speed_halo))
    share = lead_share(offsets, index_x, index_y, size_x, size_y, tiles_across, tile_height)
    weight = weight_pattern(grid_levels, coefficients, faulty_grids)
    hat = hat_matrix(HAT).astype(jnp.bfloat16)

    nodal, first_rows, last_rows, first_cols, last_cols = refine_block(
        source, slot_rank, incoming, share, weight, hat, hat.T, rows_local, cols_local, tile_height,
        capacity,
    )
    speed_halo, nodal = lax.optimization_barrier((speed_halo, nodal))
    speed, rim_speed = spread(velocity_x, velocity_y, *speed_halo)
    above, below = exchange(first_rows, last_rows, "gx")
    strips = [above, below] + [side[f] for f in range(2) for side in speed_halo[:2]]
    from_left, from_right = exchange(
        jnp.concatenate([first_cols] + [strip[:, :LANES] for strip in strips], axis=1),
        jnp.concatenate([last_cols] + [strip[:, -LANES:] for strip in strips], axis=1),
        "gy",
    )
    stencil, ring_stencil = stencil_matrices()
    main = main_steps(nodal, speed, stencil, above, below)
    return rim_steps(main, nodal, rim_speed, ring_stencil, above, below, from_left, from_right)


def solution(mesh):
    return jax.shard_map(
        local,
        mesh=mesh,
        in_specs=(P(("gx", "gy"), None, None), P(), P(), P(), P(), P("gx", "gy"), P("gx", "gy")),
        out_specs=P("gx", "gy"),
        check_vma=False,
    )
```

```python
import functools

import jax
import jax.numpy as jnp
from jax import lax
from jax.experimental import pallas as pl
from jax.experimental.pallas import tpu as pltpu
from jax.sharding import PartitionSpec as P

STEPS = 2
TIME_STEP = 0.2
DIFFUSION = 0.5
HALO = 8
LANES = 128
HAT = 256
VMEM_LIMIT = 24 << 20
PACK_LIMIT = 60 << 20
REFINE_LIMIT = 40 << 20


def pack_kernel(
    tiles_across, capacity, owner_ref, owned_ref, outgoing_ref, staged, wide, leads, offsets, used,
    sem_in, sem_out, sem_lead, sem_owner,
):
    count, tile_rows, _ = owned_ref.shape
    messages = outgoing_ref.shape[0]
    size = 2 * tile_rows
    groups = sem_in.shape[0]
    per_group = count // groups

    def arrival(g):
        part = pl.ds(g * per_group, per_group)
        return pltpu.make_async_copy(owned_ref.at[part], staged.at[part], sem_in.at[g])

    head = pltpu.make_async_copy(owner_ref.at[pl.ds(0, count)], offsets, sem_owner)
    head.start()
    for g in range(groups):
        arrival(g).start()
    own_index = lax.axis_index("gx") * lax.axis_size("gy") + lax.axis_index("gy")

    def clear(m, carry):
        used[m] = 0
        return carry

    lax.fori_loop(0, messages, clear, 0, unroll=8)
    head.wait()
    for g in range(groups):
        arrival(g).wait()

        def place(i, carry, g=g):
            k = g * per_group + i
            wide[k, :tile_rows, :] = staged[k, :, :LANES]
            wide[k, tile_rows:, :] = staged[k, :, LANES:]
            offset = offsets[k]
            rank = used[offset]
            used[offset] = rank + 1
            target = lax.rem(own_index - offset + messages, messages)
            row = pl.multiple_of(rank * size, size)
            pltpu.make_async_copy(
                wide.at[k], outgoing_ref.at[target, pl.ds(row, size), :], sem_out
            ).start()
            return carry

        lax.fori_loop(0, per_group, place, 0, unroll=8)

    rows = []
    for ky in range(tiles_across):
        rows += [staged[ky, 0:1, :LANES], staged[ky, 0:1, LANES:]]
    per_part = LANES // tile_rows
    for part in range(count // tiles_across // per_part):
        columns = [staged[(part * per_part + t) * tiles_across, :, :LANES] for t in range(per_part)]
        rows.append(jnp.concatenate(columns, axis=0).T[0:1])
    rows += [rows[0]] * 4
    lead = jnp.concatenate(rows, axis=0)

    def address(m, carry):
        leads[m] = lead
        return carry

    lax.fori_loop(0, messages, address, 0, unroll=8)
    to_all = pltpu.make_async_copy(
        leads, outgoing_ref.at[:, pl.ds(size * capacity, lead.shape[0]), :], sem_lead
    )
    to_all.start()
    to_all.wait()
    pltpu.make_async_copy(wide, wide, sem_out).wait()


def pack(tile_owner, owned, messages, capacity, tiles_across):
    count, tile_rows, _ = owned.shape
    lead_rows = 2 * tiles_across + count // tiles_across * tile_rows // LANES + 4
    anywhere = pl.BlockSpec(memory_space=pl.ANY)
    return pl.pallas_call(
        functools.partial(pack_kernel, tiles_across, capacity),
        out_shape=jax.ShapeDtypeStruct(
            (messages, capacity * tile_rows * 2 + lead_rows, LANES), owned.dtype
        ),
        in_specs=[anywhere, anywhere],
        out_specs=anywhere,
        scratch_shapes=[
            pltpu.VMEM(owned.shape, owned.dtype),
            pltpu.VMEM((count, 2 * tile_rows, LANES), owned.dtype),
            pltpu.VMEM((messages, lead_rows, LANES), owned.dtype),
            pltpu.SMEM((count,), jnp.int32),
            pltpu.SMEM((messages,), jnp.int32),
            pltpu.SemaphoreType.DMA((8,)),
            pltpu.SemaphoreType.DMA,
            pltpu.SemaphoreType.DMA,
            pltpu.SemaphoreType.DMA,
        ],
        compiler_params=pltpu.CompilerParams(vmem_limit_bytes=PACK_LIMIT),
        name="pack_tiles",
    )(tile_owner, owned)


def split_dot(left, right, split_left):
    value = left if split_left else right
    high = value.astype(jnp.bfloat16)
    low = (value - high.astype(jnp.float32)).astype(jnp.bfloat16)
    both = jnp.concatenate([high, low], axis=1 if split_left else 0)
    pair = (both, right) if split_left else (left, both)
    return jnp.dot(*pair, preferred_element_type=jnp.float32)


def refine_kernel(
    tiles_across, tile_rows, capacity, source_ref, rank_ref, incoming_ref, share_ref, weight_ref,
    hat_x_ref, hat_y_ref, nodal_ref, first_rows_ref, last_rows_ref, left_ref, right_ref,
    block, edge, staged, leads, sem_tile, sem_lead,
):
    height = nodal_ref.shape[1]
    tiles_down = height // tile_rows
    row_parts = 2 * tiles_across
    col_parts = height // LANES
    lead_row = 2 * tile_rows * capacity
    lead_size = share_ref.shape[2]
    tile_weight = jnp.concatenate([weight_ref[...]] * (tile_rows // 8), axis=0)
    size = 2 * tile_rows
    groups = sem_tile.shape[0]
    per_group = tiles_down * tiles_across // groups
    lead_copy = pltpu.make_async_copy(
        incoming_ref.at[:, pl.ds(lead_row, lead_size), :], leads, sem_lead
    )
    lead_copy.start()
    for g in range(groups):

        def fetch(i, carry, g=g):
            k = g * per_group + i
            row = pl.multiple_of(rank_ref[k] * size, size)
            pltpu.make_async_copy(
                incoming_ref.at[source_ref[k], pl.ds(row, size), :], staged.at[k], sem_tile.at[g]
            ).start()
            return carry

        lax.fori_loop(0, per_group, fetch, 0, unroll=8)
    lead_copy.wait()

    def collect(m, sums):
        lead = leads[m]
        return tuple(total + share_ref[i, m] * lead for i, total in enumerate(sums))

    zero = jnp.zeros((lead_size, LANES), jnp.float32)
    own_lead, next_lead = lax.fori_loop(0, leads.shape[0], collect, (zero, zero), unroll=8)

    weight = weight_ref[...]
    lane = lax.broadcasted_iota(jnp.int32, (1, LANES), 1)
    corner_base = row_parts + col_parts
    corner = lambda x: weight[0:1, 0:1] * jnp.where(
        lane == 0,
        own_lead[corner_base + 2 * x : corner_base + 2 * x + 1, 0:1],
        own_lead[corner_base + 2 * x + 1 : corner_base + 2 * x + 2, 0:1],
    )
    for part in range(col_parts):
        pair = jnp.concatenate(
            [
                own_lead[row_parts + part : row_parts + part + 1],
                next_lead[row_parts + part : row_parts + part + 1],
                jnp.zeros((LANES - 2, LANES), jnp.float32),
            ],
            axis=0,
        ).T
        edge[part * LANES : (part + 1) * LANES, :] = (
            pair.reshape(LANES // 8, 8, LANES) * weight[:, 0:1][None]
        ).reshape(LANES, LANES)

    row_id = lax.broadcasted_iota(jnp.int32, (HAT, HAT), 0)
    lane_id = lax.broadcasted_iota(jnp.int32, (HAT, HAT), 1)
    ramp_rows = row_id.astype(jnp.float32) * (1.0 / HAT)
    ramp_lanes = lane_id.astype(jnp.float32) * (1.0 / HAT)

    def refine_down(target, lanes, own, after):
        width = own.shape[1]
        middle = target[HAT : HAT + 1, lanes] + 0.5 * (own + after)
        for part, (first, last) in enumerate(((own, middle), (middle, after))):
            rows = slice(part * HAT, (part + 1) * HAT)
            values = jnp.where(row_id[:, :width] == 0, first, target[rows, lanes])
            target[rows, lanes] = split_dot(hat_x_ref[...], values, False) + ramp_rows[:, :width] * last

    refine_down(edge, slice(0, LANES), corner(0), corner(1))

    def place(kx, carry):
        row = pl.multiple_of(kx * tile_rows, tile_rows)
        for ky in range(tiles_across):
            for part in range(2):
                block[pl.ds(row, tile_rows), (2 * ky + part) * LANES : (2 * ky + part + 1) * LANES] = (
                    staged[kx * tiles_across + ky, part * tile_rows : (part + 1) * tile_rows, :]
                    * tile_weight
                )
        return carry

    for g in range(groups):
        part = staged.at[pl.ds(g * per_group, per_group)]
        pltpu.make_async_copy(part, part, sem_tile.at[g]).wait()
        lax.fori_loop(
            g * tiles_down // groups, (g + 1) * tiles_down // groups, place, 0, unroll=2
        )
    line = lambda lead, ky: (
        jnp.concatenate([lead[2 * ky : 2 * ky + 1], lead[2 * ky + 1 : 2 * ky + 2]], axis=1)
        * jnp.concatenate([weight[0:1]] * 2, axis=1)
    )
    for ky in range(tiles_across):
        refine_down(
            block, slice(ky * HAT, (ky + 1) * HAT), line(own_lead, ky), line(next_lead, ky)
        )
    for part in range(height // HAT):
        rows = slice(part * HAT, (part + 1) * HAT)
        ends = [edge[rows, 0:1], None, None, None, edge[rows, 1:2]]
        for middle, before, after in ((2, 0, 4), (1, 0, 2), (3, 2, 4)):
            ends[middle] = block[rows, middle * HAT : middle * HAT + 1] + 0.5 * (
                ends[before] + ends[after]
            )
        for ky in range(tiles_across):
            values = jnp.where(lane_id == 0, ends[ky], block[rows, ky * HAT : (ky + 1) * HAT])
            result = split_dot(values, hat_y_ref[...], True) + ramp_lanes * ends[ky + 1]
            nodal_ref[2 * ky, rows, :] = result[:, :LANES]
            nodal_ref[2 * ky + 1, rows, :] = result[:, LANES:]
            columns = slice(ky * HAT, (ky + 1) * HAT)
            if part == 0:
                first_rows_ref[:, columns] = result[:HALO]
            if part == height // HAT - 1:
                last_rows_ref[:, columns] = result[-HALO:]
            if ky == 0:
                left_ref[:, rows] = result[:, :LANES].T[:HALO]
            if ky == tiles_across - 1:
                right_ref[:, rows] = result[:, LANES:].T[-HALO:]


def refine_block(source, rank, incoming, share, weight, hat_x, hat_y, height, width, tile_rows, capacity):
    vmem = pl.BlockSpec(memory_space=pltpu.VMEM)
    smem = pl.BlockSpec(memory_space=pltpu.SMEM)
    shapes = [(width // LANES, height, LANES)] + [(HALO, width)] * 2 + [(HALO, height)] * 2
    return pl.pallas_call(
        functools.partial(refine_kernel, width // HAT, tile_rows, capacity),
        out_shape=[jax.ShapeDtypeStruct(shape, jnp.float32) for shape in shapes],
        in_specs=[smem, smem, pl.BlockSpec(memory_space=pltpu.HBM)] + [vmem] * 4,
        out_specs=[vmem] * len(shapes),
        scratch_shapes=[
            pltpu.VMEM((height, width), jnp.float32),
            pltpu.VMEM((height, LANES), jnp.float32),
            pltpu.VMEM((source.shape[0], 2 * tile_rows, LANES), jnp.float32),
            pltpu.VMEM((incoming.shape[0], share.shape[2], LANES), jnp.float32),
            pltpu.SemaphoreType.DMA((4,)),
            pltpu.SemaphoreType.DMA,
        ],
        compiler_params=pltpu.CompilerParams(vmem_limit_bytes=REFINE_LIMIT),
        name="refine_block",
    )(source, rank, incoming, share, weight, hat_x, hat_y)


def split(value):
    high = value.astype(jnp.bfloat16)
    return high, (value - high.astype(jnp.float32)).astype(jnp.bfloat16)


def heun_loops(
    field, middle, speed, height, chunk, last_chunk, make_across, store_last, after_last
):
    count = field.shape[0]
    scale = TIME_STEP * DIFFUSION / 12.0

    def advance(source, start, size, store):
        across_of = make_across(source, start, size)
        for t in range(count):
            across = across_of(t)
            one_below = source[t, pl.ds(start - 1, size), :]
            one_above = source[t, pl.ds(start + 1, size), :]
            two_below = source[t, pl.ds(start - 2, size), :]
            two_above = source[t, pl.ds(start + 2, size), :]
            curve = 16.0 * (one_above + one_below) - (two_above + two_below) + across[:, :LANES]
            slope = 8.0 * (one_above - one_below) - (two_above - two_below)
            result = scale * curve - speed[0, t, pl.ds(start, size), :] * slope
            store(t, result - speed[1, t, pl.ds(start, size), :] * across[:, LANES:])

    def first_half(c, carry):
        start = pl.multiple_of(HALO + c * chunk, HALO)

        def store(t, result):
            middle[t, pl.ds(start, chunk), :] = result

        advance(field, start, chunk, store)
        return carry

    def second_half(c, carry):
        start = pl.multiple_of(HALO + c * chunk, HALO)

        def store(t, result):
            field[t, pl.ds(start, chunk), :] = 0.5 * (field[t, pl.ds(start, chunk), :] + result)

        advance(middle, start, chunk, store)
        return carry

    def last_half(c, carry):
        start = pl.multiple_of(2 * HALO + c * last_chunk, HALO)
        place = pl.ds(pl.multiple_of(c * last_chunk, HALO), last_chunk)

        def store(t, result):
            store_last(t, place, 0.5 * (field[t, pl.ds(start, last_chunk), :] + result))

        advance(middle, start, last_chunk, store)
        after_last(place)
        return carry

    extended = (height + 2 * HALO) // chunk
    for step in range(STEPS):
        lax.fori_loop(0, extended, first_half, 0)
        if step < STEPS - 1:
            lax.fori_loop(0, extended, second_half, 0)
    lax.fori_loop(0, height // last_chunk, last_half, 0)


def largest_chunk(rows, limit):
    return max(size for size in range(16, limit + 1, 16) if rows % size == 0)


def chunks(height, limit):
    return largest_chunk(height + 2 * HALO, limit), largest_chunk(height, limit)


def main_kernel(
    nodal_ref, speed, stencil_ref, rows_above, rows_below, out_ref, field, middle, result_ref, sem
):
    tiles, height, _ = nodal_ref.shape
    first, end = 2 * HALO, 2 * HALO + height
    for t in range(tiles):
        lanes = slice(t * LANES, (t + 1) * LANES)
        field[t, first:end, :] = nodal_ref[t]
        field[t, HALO:first, :] = rows_above[:, lanes]
        field[t, end : end + HALO, :] = rows_below[:, lanes]

    def make_across(source, start, size):
        parts = {}
        lane = lax.broadcasted_iota(jnp.int32, (size, LANES), 1)

        def part(t):
            if t not in parts:
                parts[t] = split(source[t, pl.ds(start, size), :])
            return parts[t]

        def inputs(t):
            before, after = part((t - 1) % tiles), part((t + 1) % tiles)
            around = [jnp.where(lane >= LANES // 2, b, a) for b, a in zip(before, after)]
            return jnp.concatenate([*part(t), *around], axis=1)

        across = jnp.dot(
            jnp.concatenate([inputs(t) for t in range(tiles)], axis=0),
            stencil_ref[...],
            preferred_element_type=jnp.float32,
        )
        return lambda t: across[t * size : (t + 1) * size]

    def store_last(t, place, value):
        result_ref[place, t * LANES : (t + 1) * LANES] = value

    def after_last(place):
        pltpu.make_async_copy(result_ref.at[place], out_ref.at[place], sem).start()

    heun_loops(
        field, middle, speed, height, *chunks(height, 192), make_across, store_last, after_last
    )
    pltpu.make_async_copy(result_ref, out_ref, sem).wait()


def main_steps(nodal, speed, stencil, above, below):
    tiles, height, _ = nodal.shape
    vmem = pl.BlockSpec(memory_space=pltpu.VMEM)
    extended = (tiles, height + 4 * HALO, LANES)
    cells = height * tiles * LANES
    return pl.pallas_call(
        main_kernel,
        out_shape=jax.ShapeDtypeStruct((height, tiles * LANES), jnp.float32),
        in_specs=[vmem] * 5,
        out_specs=pl.BlockSpec(memory_space=pl.ANY),
        scratch_shapes=[
            pltpu.VMEM(extended, jnp.float32),
            pltpu.VMEM(extended, jnp.float32),
            pltpu.VMEM((height, tiles * LANES), jnp.float32),
            pltpu.SemaphoreType.DMA,
        ],
        compiler_params=pltpu.CompilerParams(vmem_limit_bytes=VMEM_LIMIT),
        cost_estimate=pl.CostEstimate(
            flops=4 * 2 * cells * 8 * LANES, bytes_accessed=16 * cells, transcendentals=0
        ),
        name="heun_main",
    )(nodal, speed, stencil, above, below)


def quarters(first, last, after, before):
    quarter = lax.broadcasted_iota(jnp.int32, first.shape, 1) // (LANES // 4)
    inner = jnp.where(quarter == 0, first, pltpu.roll(last, LANES // 2, axis=1))
    return jnp.where(quarter < 2, inner, jnp.where(quarter == 2, after, before))


def outer_columns(before, after):
    height = before.shape[1]
    low = jnp.zeros((LANES // 2, height), jnp.float32)
    high = jnp.zeros((LANES // 2 - 2 * HALO, height), jnp.float32)
    return jnp.concatenate([low, after, high, before], axis=0).T


def spread_kernel(
    x_ref, y_ref, above_ref, below_ref, left_ref, right_ref, speed_ref, rim_ref
):
    height, width = x_ref.shape
    first, end = 2 * HALO, 2 * HALO + height
    scale = TIME_STEP / 12.0
    for f, velocity in enumerate((x_ref, y_ref)):
        for t in range(width // LANES):
            lanes = slice(t * LANES, (t + 1) * LANES)
            speed_ref[f, t, first:end, :] = velocity[:, lanes] * scale
            speed_ref[f, t, HALO:first, :] = above_ref[f, :, lanes] * scale
            speed_ref[f, t, end : end + HALO, :] = below_ref[f, :, lanes] * scale
        ends = lambda rows: (rows[:, :LANES], rows[:, width - LANES :])
        outer = outer_columns(left_ref[f], right_ref[f])
        rim_ref[f, 0, first:end, :] = quarters(*ends(velocity), outer, outer) * scale
        for received, rows in ((above_ref, slice(HALO, first)), (below_ref, slice(end, end + HALO))):
            inner = ends(received[f])
            rim_ref[f, 0, rows, :] = quarters(*inner, *inner) * scale


def spread(x, y, *halo):
    height, width = x.shape
    vmem = pl.BlockSpec(memory_space=pltpu.VMEM)
    rows = height + 4 * HALO
    return pl.pallas_call(
        spread_kernel,
        out_shape=[
            jax.ShapeDtypeStruct((2, width // LANES, rows, LANES), jnp.float32),
            jax.ShapeDtypeStruct((2, 1, rows, LANES), jnp.float32),
        ],
        in_specs=[vmem] * (2 + len(halo)),
        out_specs=[vmem, vmem],
        compiler_params=pltpu.CompilerParams(vmem_limit_bytes=VMEM_LIMIT),
        cost_estimate=pl.CostEstimate(
            flops=4 * height * width, bytes_accessed=20 * height * width, transcendentals=0
        ),
        name="spread_velocity",
    )(x, y, *halo)


def rim_kernel(
    main_ref, nodal_ref, rim_ref, stencil_ref, rows_above, rows_below, from_left, from_right, out_ref,
    field, middle, speed, result_ref, sem,
):
    tiles, height, _ = nodal_ref.shape
    width = tiles * LANES
    first, end = 2 * HALO, 2 * HALO + height
    sides = (slice(0, LANES), slice(width - LANES, width))
    fetches = [
        pltpu.make_async_copy(main_ref.at[:, pl.ds(side.start, LANES)], result_ref.at[i], sem.at[i])
        for i, side in enumerate(sides)
    ]
    for fetch in fetches:
        fetch.start()

    def corner(received, k):
        return received[:, height + k * LANES : height + (k + 1) * LANES]

    ends = lambda rows: (rows[:, sides[0]], rows[:, sides[1]])
    outer_corner = lambda k: (
        pltpu.roll(corner(from_right, k), LANES // 2, axis=1), corner(from_left, k)
    )
    outer = outer_columns(from_left[:, :height], from_right[:, :height])
    field[0, first:end, :] = quarters(nodal_ref[0], nodal_ref[tiles - 1], outer, outer)
    field[0, HALO:first, :] = quarters(*ends(rows_above), *outer_corner(0))
    field[0, end : end + HALO, :] = quarters(*ends(rows_below), *outer_corner(1))
    lane = lax.broadcasted_iota(jnp.int32, (HALO, LANES), 1)
    for f in range(2):
        speed[f, 0, first:end, :] = rim_ref[f, 0, first:end, :]
        for k, rows in enumerate((slice(HALO, first), slice(end, end + HALO))):
            after, before = outer_corner(2 + 2 * f + k)
            outside = jnp.where(lane < 3 * LANES // 4, after, before) * (TIME_STEP / 12.0)
            speed[f, 0, rows, :] = jnp.where(lane < LANES // 2, rim_ref[f, 0, rows, :], outside)
    for fetch in fetches:
        fetch.wait()

    def make_across(source, start, size):
        def across_of(t):
            return jnp.dot(
                jnp.concatenate(split(source[t, pl.ds(start, size), :]), axis=1),
                stencil_ref[...],
                preferred_element_type=jnp.float32,
            )

        return across_of

    def store_last(t, place, value):
        lane = lax.broadcasted_iota(jnp.int32, value.shape, 1)
        result_ref[0, place, :] = jnp.where(lane < HALO, value, result_ref[0, place, :])
        result_ref[1, place, :] = jnp.where(
            lane >= LANES - HALO, pltpu.roll(value, LANES // 2, axis=1), result_ref[1, place, :]
        )

    def after_last(place):
        for i, side in enumerate(sides):
            pltpu.make_async_copy(
                result_ref.at[i, place], out_ref.at[place, pl.ds(side.start, LANES)], sem.at[i]
            ).start()

    heun_loops(
        field, middle, speed, height, *chunks(height, 264), make_across, store_last, after_last
    )
    for i, side in enumerate(sides):
        pltpu.make_async_copy(
            result_ref.at[i], out_ref.at[:, pl.ds(side.start, LANES)], sem.at[i]
        ).wait()


def rim_steps(main, nodal, speed, stencil, *halo):
    _, height, _ = nodal.shape
    vmem = pl.BlockSpec(memory_space=pltpu.VMEM)
    anywhere = pl.BlockSpec(memory_space=pl.ANY)
    extended = (1, height + 4 * HALO, LANES)
    return pl.pallas_call(
        rim_kernel,
        out_shape=jax.ShapeDtypeStruct(main.shape, jnp.float32),
        in_specs=[anywhere] + [vmem] * (3 + len(halo)),
        out_specs=anywhere,
        input_output_aliases={0: 0},
        scratch_shapes=[
            pltpu.VMEM(extended, jnp.float32),
            pltpu.VMEM(extended, jnp.float32),
            pltpu.VMEM((2,) + extended, jnp.float32),
            pltpu.VMEM((2, height, LANES), jnp.float32),
            pltpu.SemaphoreType.DMA((2,)),
        ],
        compiler_params=pltpu.CompilerParams(vmem_limit_bytes=VMEM_LIMIT),
        name="heun_rim",
    )(main, nodal, speed, stencil, *halo)


def edges_kernel(*refs):
    first_rows, last_rows, first_cols, last_cols = refs[8:]
    for f in range(2):
        top, bottom, left, right = refs[4 * f : 4 * f + 4]
        first_rows[f] = top[...]
        last_rows[f] = bottom[...]
        first_cols[f] = left[...].T[:HALO]
        last_cols[f] = right[...].T[-HALO:]


def edges(x, y):
    height, width = x.shape
    specs = [
        pl.BlockSpec((HALO, width), lambda i: (0, 0)),
        pl.BlockSpec((HALO, width), lambda i: (height // HALO - 1, 0)),
        pl.BlockSpec((height, LANES), lambda i: (0, 0)),
        pl.BlockSpec((height, LANES), lambda i: (0, width // LANES - 1)),
    ]
    shapes = [(2, HALO, width)] * 2 + [(2, HALO, height)] * 2
    return pl.pallas_call(
        edges_kernel,
        grid=(1,),
        out_shape=[jax.ShapeDtypeStruct(shape, jnp.float32) for shape in shapes],
        in_specs=specs * 2,
        out_specs=[pl.BlockSpec(shape, lambda i: (0, 0, 0)) for shape in shapes],
        name="velocity_edges",
    )(*[x] * 4, *[y] * 4)


def stencil_entries(shift, column):
    distance = jnp.abs(shift)
    centre = 12.0 / (TIME_STEP * DIFFUSION) - 60.0
    curve = jnp.where(distance == 1, 16.0, jnp.where(distance == 2, -1.0, 0.0))
    curve = jnp.where(distance == 0, centre, curve)
    slope = jnp.where(distance == 1, 8.0, jnp.where(distance == 2, -1.0, 0.0)) * jnp.sign(
        shift
    ).astype(jnp.float32)
    return jnp.where(column < LANES, curve, slope).astype(jnp.bfloat16)


def stencil_matrices():
    row = lax.broadcasted_iota(jnp.int32, (4 * LANES, 2 * LANES), 0)
    column = lax.broadcasted_iota(jnp.int32, (4 * LANES, 2 * LANES), 1)
    lane = row % LANES
    outside = jnp.where(lane < LANES // 2, lane + LANES, lane - LANES)
    shift = jnp.where(row < 2 * LANES, lane, outside) - column % LANES
    ring = lane - column % LANES
    ring = jnp.where(ring > LANES // 2, ring - LANES, jnp.where(ring < -LANES // 2, ring + LANES, ring))
    return stencil_entries(shift, column), stencil_entries(ring, column)[: 2 * LANES]


def hat_matrix(size):
    place = lax.broadcasted_iota(jnp.int32, (size, size), 0)
    node = lax.broadcasted_iota(jnp.int32, (size, size), 1)
    return jnp.where(node == 0, 1.0 - place.astype(jnp.float32) / size, hat_value(node, place))


def hat_value(node, place):
    spacing = jnp.maximum(node & (-node), 1).astype(jnp.float32)
    return jnp.maximum(0.0, 1.0 - jnp.abs(place - node).astype(jnp.float32) / spacing)


def coarse_share(node, place):
    return jnp.where(node == 0, 1.0, hat_value(node, place))


def weight_pattern(grid_levels, coefficients, faulty_grids):
    grid_ids = jnp.arange(coefficients.shape[0], dtype=jnp.int32)
    alive = jnp.all(faulty_grids[None, :] != grid_ids[:, None], axis=1)
    share = jnp.where(alive, coefficients, 0).astype(jnp.float32)
    row = lax.broadcasted_iota(jnp.int32, (8, LANES), 0)[None]
    lane = lax.broadcasted_iota(jnp.int32, (8, LANES), 1)[None]
    mask_x = (jnp.int32(1) << grid_levels[:, 0]) - 1
    mask_y = (jnp.int32(1) << grid_levels[:, 1]) - 1
    covered = ((row & mask_x[:, None, None]) == 0) & ((lane & mask_y[:, None, None]) == 0)
    return jnp.sum(jnp.where(covered, share[:, None, None], 0.0), axis=0)


def exchange(first, last, axis):
    size = lax.axis_size(axis)
    even = lax.axis_index(axis) % 2 == 0
    inner = [(i, i ^ 1) for i in range(size)]
    outer = [((i + 1) % size, ((i ^ 1) + 1) % size) for i in range(size)]
    by_inner = lax.ppermute(jnp.where(even, last, first), axis, inner)
    by_outer = lax.ppermute(jnp.where(even, first, last), axis, outer)
    return jnp.where(even, by_outer, by_inner), jnp.where(even, by_inner, by_outer)


def lead_share(offsets, index_x, index_y, size_x, size_y, tiles_across, tile_height):
    devices = size_x * size_y
    row_parts = 2 * tiles_across
    by_row = jnp.repeat(offsets[:tiles_across], 2)[:, None]
    by_col = jnp.repeat(offsets[::tiles_across], tile_height).reshape(-1, LANES)
    spread_row = jnp.broadcast_to(by_row, (row_parts, LANES))
    spread_corner = jnp.broadcast_to(offsets[0], (4, LANES))
    table = jnp.concatenate([spread_row, by_col, spread_corner], axis=0)
    owner = lax.broadcasted_iota(jnp.int32, (devices, 1, 1), 0)
    block = (owner - table[None]) % devices
    x, y = block // size_y, block % size_y
    line = lax.broadcasted_iota(jnp.int32, (1, table.shape[0], 1), 1)
    corner = line - (table.shape[0] - 4)
    shares = []
    for by in range(2):
        rows = jnp.where(y == index_y, coarse_share(x, index_x + by), 0.0)
        cols = jnp.where(x == index_x, coarse_share(y, index_y + by), 0.0)
        corners = coarse_share(x, index_x + corner // 2) * coarse_share(y, index_y + corner % 2)
        shares.append(
            jnp.where(line < row_parts, rows, jnp.where(corner < 0, cols, corners))
        )
    return jnp.stack(shares)


def local(
    owned_surplus, tile_owner, grid_levels, coefficients, faulty_grids, velocity_x, velocity_y
):
    slot_count, tile_height, tile_width = owned_surplus.shape
    rows_local, cols_local = velocity_x.shape
    size_x = lax.axis_size("gx")
    size_y = lax.axis_size("gy")
    device_count = size_x * size_y
    capacity = 2 * slot_count // device_count
    tiles_across = cols_local // tile_width
    index_x = lax.axis_index("gx")
    index_y = lax.axis_index("gy")
    own_index = index_x * size_y + index_y
    offsets = tile_owner[:slot_count]
    positions = jnp.arange(slot_count, dtype=jnp.int32)
    same_offset = offsets[:, None] == offsets[None, :]
    earlier = positions[None, :] < positions[:, None]
    slot_rank = jnp.sum((same_offset & earlier).astype(jnp.int32), axis=1)
    source = (own_index + offsets) % device_count
    outgoing = pack(tile_owner, owned_surplus, device_count, capacity, tiles_across)
    incoming = lax.all_to_all(outgoing, ("gx", "gy"), split_axis=0, concat_axis=0, tiled=True)

    first_rows, last_rows, first_cols, last_cols = edges(velocity_x, velocity_y)
    speed_halo = (
        *exchange(first_rows, last_rows, "gx"),
        *exchange(first_cols, last_cols, "gy"),
    )
    incoming, speed_halo = lax.optimization_barrier((incoming, speed_halo))
    share = lead_share(offsets, index_x, index_y, size_x, size_y, tiles_across, tile_height)
    weight = weight_pattern(grid_levels, coefficients, faulty_grids)
    hat = hat_matrix(HAT).astype(jnp.bfloat16)
    hat_x, hat_y = jnp.concatenate([hat, hat], axis=1), jnp.concatenate([hat.T, hat.T], axis=0)

    nodal, first_rows, last_rows, first_cols, last_cols = refine_block(
        source, slot_rank, incoming, share, weight, hat_x, hat_y, rows_local, cols_local, tile_height,
        capacity,
    )
    speed_halo, nodal = lax.optimization_barrier((speed_halo, nodal))
    speed, rim_speed = spread(velocity_x, velocity_y, *speed_halo)
    above, below = exchange(first_rows, last_rows, "gx")
    strips = [above, below] + [side[f] for f in range(2) for side in speed_halo[:2]]
    from_left, from_right = exchange(
        jnp.concatenate([first_cols] + [strip[:, :LANES] for strip in strips], axis=1),
        jnp.concatenate([last_cols] + [strip[:, -LANES:] for strip in strips], axis=1),
        "gy",
    )
    stencil, ring_stencil = stencil_matrices()
    main = main_steps(nodal, speed, stencil, above, below)
    return rim_steps(main, nodal, rim_speed, ring_stencil, above, below, from_left, from_right)


def solution(mesh):
    return jax.shard_map(
        local,
        mesh=mesh,
        in_specs=(P(("gx", "gy"), None, None), P(), P(), P(), P(), P("gx", "gy"), P("gx", "gy")),
        out_specs=P("gx", "gy"),
        check_vma=False,
    )
```
